256 devices in a mesh: cls: 2 (over y_hi), dom: 16 (over y_lo, x, core), orient: 8 (over z).
Axes of the slice: x: 4, y: 4 (y_hi: 2, y_lo: 2; y = y_hi * 2 + y_lo), z: 8, core: 2. Of those that a mesh axis runs over, the one named last changes fastest.
Arguments:
- references: bfloat16 [2, 8, 8, 32768], P(None, 'cls', None, ('dom', 'orient')), may hold values from -2 to 2
- images: bfloat16 [2, 2048, 32768], P(None, ('dom', 'orient')), may hold values from -16 to 16
- orient_lists: int32 [2048, 1], P(('dom', 'orient')), may hold values from 0 to 7; in each aligned block of 16 rows (0 to 15, 16 to 31, ...) at most 3 rows name the same one
- shift_ids: int32 [2048, 1], P(('dom', 'orient')), may hold values from 0 to 63
- fixed_weights: float32 [2048, 1], P(('dom', 'orient')), may hold values from 0.2 to 2
Outputs:
- class_prob: float32 [2048, 8], P(('dom', 'orient'), 'cls')
- volume: float32 [2, 8, 8, 32768], P(None, 'cls', 'orient', 'dom')
The draws below stay inside these ranges and needn't reach their ends.
Inputs may be any that keep to these rules, and one draw needn't show every extreme that they name: `orient_lists`: within the rows of one device (16 particles), no orientation bin is listed by more than 3 particles, a bound that some block reaches.
All inputs are finite; a program needn't handle non-finite values.
Results may differ from the reference program's by a relative error of at most 0.02.
Values may be sent and summed in bfloat16 or wider, within the bound.
A program may use at most 320 MiB of HBM per device.

```python
import math
import jax
import jax.numpy as jnp
import numpy as np
from jax import lax

IMG = 256
PIX = 32768
TX = 8
TY = 8
SHIFTS = 64
CLASSES = 8
ORIENTS = 8
PART_DEV = 16
PARTICLES = 2048
S = 1
MOST = 3


def ref_table(key):
    values = jax.random.normal(jax.random.fold_in(key, 11), (2, CLASSES, ORIENTS, PIX), jnp.float32)
    return jnp.clip(values, -6.0, 6.0) * (3.0 / math.sqrt(2.0 * PIX))


def draw_references(key, part):
    return ref_table(key).astype(jnp.bfloat16)


def draw_images(key, part):
    noise_field = jax.random.normal(jax.random.fold_in(key, 12), (2, PARTICLES, PIX), jnp.float32)
    noise_field = jnp.clip(noise_field, -6.0, 6.0)
    return noise_field.astype(jnp.bfloat16)


def set_ends(drawn, stream_key, smallest, top_value):
    longest = drawn.shape.index(max(drawn.shape))
    spots = []
    for shift in (0, 1):
        where = [jax.random.randint(jax.random.fold_in(stream_key, axis), (), 0, length) for axis, length in enumerate(drawn.shape)]
        where[longest] = (where[longest] + shift) % drawn.shape[longest]
        spots.append(tuple(where))
    return drawn.at[spots[0]].set(smallest).at[spots[1]].set(top_value)


def steps_of(stream_key, dims, pieces, least, top_value):
    def one(axis_at, blocks):
        steps = jax.random.uniform(jax.random.fold_in(jax.random.fold_in(stream_key, 6), axis_at), (blocks,), jnp.float32, least / len(pieces), top_value / len(pieces))
        return jnp.repeat(jnp.exp(steps), dims[axis_at] // blocks).reshape((-1,) + (1,) * (len(dims) - axis_at - 1))

    loudness = one(*pieces[0])
    for cut in pieces[1:]:
        loudness = loudness * one(*cut)
    return loudness


def routed_block(stream_key, own, number, rows, number_of, top, reach, slope):
    sequence = jax.random.permutation(stream_key, number_of)
    packed, ordinary = portions_of(number_of, rows * top, reach, slope, True), portions_of(number_of, rows * top, reach, slope, False)
    places = jnp.arange(number_of)

    def named(sizes, turn):
        used = int((sizes > 0).sum())
        fixed = max(1, used // 4)
        moved = fixed + (places - fixed + turn * (used - fixed)) % max(1, number_of - fixed)
        return jnp.zeros((number_of,), jnp.int32).at[sequence[jnp.where(places < fixed, places, moved)]].set(jnp.asarray(sizes, jnp.int32))

    sizes = jnp.where(number % 4 == 0, named(packed, number // 4), named(ordinary, number - number // 4 - 1))
    mixed = jax.random.permutation(jax.random.fold_in(own, 3), number_of)
    donor, taker = mixed[0:number_of // 2 * 2:2], mixed[1:number_of // 2 * 2:2]
    margin = jnp.minimum(sizes[donor] - 1, reach - sizes[taker]) // 2
    margin = jnp.where((donor == sequence[0]) | (taker == sequence[0]) | (sizes[taker] == 0), 0, jnp.maximum(margin, 0))
    moved = jax.random.randint(jax.random.fold_in(own, 4), (number_of // 2,), 0, 1 << 20) % (margin + 1)
    sizes = sizes.at[donor].add(-moved).at[taker].add(moved)
    labels = jnp.searchsorted(jnp.cumsum(sizes), jnp.arange(rows * top), side="right").astype(jnp.int32)
    grid = labels.reshape(top, rows).T
    grid = grid[jax.random.permutation(jax.random.fold_in(own, 1), rows)]
    turn = jax.random.randint(jax.random.fold_in(own, 2), (rows, 1), 0, top)
    return jnp.take_along_axis(grid, (jnp.arange(top)[None, :] + turn) % top, axis=1)


def portions_of(amount, total, bound, slope, full):
    portions = [(1 << 20) // math.isqrt(standing ** slope) + 1 for standing in range(1, amount + 1)]
    largest = bound if full else min(bound, max(-(-total // amount), total * portions[0] // sum(portions)))
    least = 1 if total - largest >= amount - 1 else 0
    given, surplus = [largest] + [least] * (amount - 1), total - largest - least * (amount - 1)
    while surplus > 0:
        movable = [i for i in range(1, amount) if given[i] < largest] or [i for i in range(1, amount) if given[i] < bound]
        mass, remaining = sum([portions[i] for i in movable]), surplus
        for i in movable:
            more = min(bound - given[i], max(1, remaining * portions[i] // mass), surplus)
            given[i] = given[i] + more
            surplus = surplus - more
    return np.array(given)


def setup_inputs(seed: int = 0) -> dict:
    key_of = jax.random.split(jax.random.key(seed), 6)
    references = draw_references(jax.random.fold_in(key_of[5], 71), 0)
    images = draw_images(jax.random.fold_in(key_of[5], 71), 0)
    orient_lists_keys = jax.random.split(jax.random.fold_in(key_of[2], 1), PARTICLES // PART_DEV)
    orient_lists_turns = jax.random.permutation(jax.random.fold_in(key_of[2], 3), PARTICLES // PART_DEV)
    orient_lists = jax.vmap(lambda own, number: routed_block(jax.random.fold_in(key_of[2], 2), own, number, PART_DEV, ORIENTS, S, MOST, 2))(orient_lists_keys, orient_lists_turns).reshape((PARTICLES, S))
    shift_ids = set_ends(jax.random.randint(key_of[3], (PARTICLES, S), 0, SHIFTS), jax.random.fold_in(key_of[3], 1), 0, SHIFTS - 1).astype(jnp.int32)
    fixed_weights = jnp.clip(jnp.exp(math.log(2.0) - 2.3025851 * jax.random.uniform(key_of[4], (PARTICLES, S), jnp.float32) ** steps_of(key_of[4], (PARTICLES, S), ((0, 128),), -0.2, 0.2)), 0.2, 2.0)
    return dict(references=references, images=images, orient_lists=orient_lists, shift_ids=shift_ids, fixed_weights=fixed_weights)


TWO_PI = 2.0 * math.pi


def freq_ids(columns):
    freq_x = (columns % IMG - IMG // 2).astype(jnp.float32)
    freq_y = (columns // IMG).astype(jnp.float32)
    return freq_x, freq_y


def offsets(number):
    return (jnp.arange(number, dtype=jnp.int32) - number // 2).astype(jnp.float32)


def reference(references, images, orient_lists, shift_ids, fixed_weights):
    columns = jnp.arange(PIX, dtype=jnp.int32)
    freq_x, freq_y = freq_ids(columns)
    angle_x = (TWO_PI / IMG) * (offsets(TX)[:, None] * freq_x[None, :])
    angle_y = (TWO_PI / IMG) * (offsets(TY)[:, None] * freq_y[None, :])
    cosine_x, sine_x = jnp.cos(angle_x), jnp.sin(angle_x)
    cosine_y, sine_y = jnp.cos(angle_y), jnp.sin(angle_y)
    ref_re = references[0].astype(jnp.float32).reshape(CLASSES * ORIENTS, PIX)
    ref_im = references[1].astype(jnp.float32).reshape(CLASSES * ORIENTS, PIX)
    shifted_ref_re = (ref_re[None] * cosine_y[:, None] + ref_im[None] * sine_y[:, None]).astype(jnp.bfloat16).reshape(TY * CLASSES * ORIENTS, PIX)
    shifted_ref_im = (ref_im[None] * cosine_y[:, None] - ref_re[None] * sine_y[:, None]).astype(jnp.bfloat16).reshape(TY * CLASSES * ORIENTS, PIX)
    block_count = PARTICLES // PART_DEV
    orient_range = jnp.arange(ORIENTS, dtype=jnp.int32)

    def scan_step(volume, block_index):
        first_row = (block_index * PART_DEV).astype(jnp.int32)
        image_block = lax.dynamic_slice_in_dim(images, first_row, PART_DEV, 1)
        image_re = image_block[0].astype(jnp.float32)
        image_im = image_block[1].astype(jnp.float32)
        shifted_x_re = (image_re[None] * cosine_x[:, None] - image_im[None] * sine_x[:, None]).astype(jnp.bfloat16).reshape(TX * PART_DEV, PIX)
        shifted_x_im = (image_re[None] * sine_x[:, None] + image_im[None] * cosine_x[:, None]).astype(jnp.bfloat16).reshape(TX * PART_DEV, PIX)
        scores = jnp.dot(shifted_x_re, shifted_ref_re.T, preferred_element_type=jnp.float32)
        scores = scores + jnp.dot(shifted_x_im, shifted_ref_im.T, preferred_element_type=jnp.float32)
        logits = scores.reshape(TX, PART_DEV, TY, CLASSES, ORIENTS)
        global_top = jnp.max(logits, axis=(0, 2, 3, 4))
        exponent = jnp.exp(logits - global_top[None, :, None, None, None])
        totals = jnp.sum(exponent, axis=(0, 2, 3, 4))
        class_prob = jnp.sum(exponent, axis=(0, 2, 4)) / totals[:, None]
        orient_ids = lax.dynamic_slice_in_dim(orient_lists, first_row, PART_DEV, 0).reshape(PART_DEV * S)
        shift_index = lax.dynamic_slice_in_dim(shift_ids, first_row, PART_DEV, 0)
        fixed_block = lax.dynamic_slice_in_dim(fixed_weights, first_row, PART_DEV, 0)
        insert_weight = (fixed_block[:, :, None] * class_prob[:, None, :]).astype(jnp.bfloat16).reshape(PART_DEV * S, CLASSES)
        entry_x = (shift_index % TX - TX // 2).astype(jnp.float32)
        entry_y = (shift_index // TX - TY // 2).astype(jnp.float32)
        angle = (TWO_PI / IMG) * (entry_x[:, :, None] * freq_x[None, None, :] + entry_y[:, :, None] * freq_y[None, None, :])
        cosine, sine = jnp.cos(angle), jnp.sin(angle)
        row_re = (image_re[:, None, :] * cosine - image_im[:, None, :] * sine).astype(jnp.bfloat16).reshape(PART_DEV * S, PIX)
        row_im = (image_re[:, None, :] * sine + image_im[:, None, :] * cosine).astype(jnp.bfloat16).reshape(PART_DEV * S, PIX)
        row_pairs = lax.optimization_barrier(jnp.stack([row_re, row_im], 0)).astype(jnp.float32)
        onehot = (orient_ids[:, None] == orient_range[None, :]).astype(jnp.float32)
        mixing = (insert_weight.astype(jnp.float32)[:, :, None] * onehot[:, None, :]).reshape(PART_DEV * S, CLASSES * ORIENTS)
        increment = jnp.einsum("em,rej->rmj", mixing, row_pairs, precision=lax.Precision.HIGHEST)
        return volume + increment.reshape(2, CLASSES, ORIENTS, PIX), class_prob

    start_volume = jnp.zeros((2, CLASSES, ORIENTS, PIX), jnp.float32)
    volume, probs = lax.scan(scan_step, start_volume, jnp.arange(block_count, dtype=jnp.int32))
    return probs.reshape(PARTICLES, CLASSES), volume
```

```python
import math

import jax
import jax.numpy as jnp
from jax import lax
from jax.sharding import PartitionSpec as P

IMG = 256
TX = 8
TY = 8
TWO_PI = 2.0 * math.pi


def offsets(number):
    return (jnp.arange(number, dtype=jnp.int32) - number // 2).astype(jnp.float32)


def local(references, images, orient_lists, shift_ids, fixed_weights):
    here = images.shape[1]
    classes, orients = references.shape[1], references.shape[2]
    doms = lax.axis_size("dom")
    band = images.shape[2] // doms
    particles = here * doms
    held = lax.all_to_all(images, "dom", split_axis=2, concat_axis=1, tiled=True)
    piece = lax.all_gather(references, "orient", axis=3, tiled=True)
    ids = lax.all_gather(
        jnp.concatenate([orient_lists, shift_ids], axis=1), "dom", axis=0, tiled=True
    )
    orient_ids, shift_index = ids[:, 0], ids[:, 1]
    columns = jnp.arange(band, dtype=jnp.int32) + lax.axis_index("dom") * band
    freq_x = (columns % IMG - IMG // 2).astype(jnp.float32)
    freq_y = (columns // IMG).astype(jnp.float32)
    angle_x = TWO_PI / IMG * (offsets(TX)[:, None] * freq_x[None, :])
    angle_y = TWO_PI / IMG * (offsets(TY)[:, None] * freq_y[None, :])
    cx, sx, cy, sy = jnp.cos(angle_x), jnp.sin(angle_x), jnp.cos(angle_y), jnp.sin(angle_y)
    re, im = held[0].astype(jnp.float32), held[1].astype(jnp.float32)
    x_re = (re[:, None] * cx - im[:, None] * sx).astype(jnp.bfloat16).reshape(particles * TX, band)
    x_im = (re[:, None] * sx + im[:, None] * cx).astype(jnp.bfloat16).reshape(particles * TX, band)
    r_re = piece[0].reshape(classes * orients, band).astype(jnp.float32)
    r_im = piece[1].reshape(classes * orients, band).astype(jnp.float32)
    s_re = (r_re[None] * cy[:, None] + r_im[None] * sy[:, None]).astype(jnp.bfloat16)
    s_im = (r_im[None] * cy[:, None] - r_re[None] * sy[:, None]).astype(jnp.bfloat16)
    s_re = s_re.reshape(TY * classes * orients, band)
    s_im = s_im.reshape(TY * classes * orients, band)
    part = jnp.einsum("aj,bj->ab", x_re, s_re, preferred_element_type=jnp.float32)
    part = part + jnp.einsum("aj,bj->ab", x_im, s_im, preferred_element_type=jnp.float32)
    part = lax.all_to_all(
        part.reshape(doms, here * TX, -1), "dom", split_axis=0, concat_axis=0, tiled=True
    )
    logits = jnp.sum(part, axis=0).reshape(here, TX, TY, classes, orients)
    top = jnp.max(logits, axis=(1, 2, 3, 4))
    top = lax.pmax(top, "cls")
    exponent = jnp.exp(logits - top[:, None, None, None, None])
    sums = jnp.sum(exponent, axis=(1, 2, 4))
    totals = lax.psum(jnp.sum(sums, axis=1), "cls")
    class_prob = sums / totals[:, None]
    weight = (fixed_weights * class_prob).astype(jnp.bfloat16)
    weight = lax.all_gather(weight, "dom", axis=0, tiled=True)
    entry_x = (shift_index % TX - TX // 2).astype(jnp.float32)
    entry_y = (shift_index // TX - TY // 2).astype(jnp.float32)
    angle = TWO_PI / IMG * (entry_x[:, None] * freq_x[None] + entry_y[:, None] * freq_y[None])
    cosine, sine = jnp.cos(angle), jnp.sin(angle)
    row_re = (re * cosine - im * sine).astype(jnp.bfloat16)
    row_im = (re * sine + im * cosine).astype(jnp.bfloat16)
    onehot = (orient_ids[:, None] == jnp.arange(orients, dtype=jnp.int32)[None]).astype(jnp.bfloat16)
    mixing = (onehot[:, :, None] * weight[:, None, :]).reshape(particles, orients * classes)
    grown = [
        jnp.einsum("pm,pj->mj", mixing, row, preferred_element_type=jnp.float32).reshape(
            orients, 1, classes, band
        )
        for row in (row_re, row_im)
    ]
    grown = jnp.concatenate(grown, axis=1)
    grown = lax.all_to_all(grown, "orient", split_axis=0, concat_axis=0, tiled=True)
    volume = jnp.sum(grown, axis=0)[:, :, None, :]
    return (class_prob, volume)


def solution(mesh):
    in_specs = (
        P(None, "cls", None, ("dom", "orient")),
        P(None, ("dom", "orient"), None),
        P(("dom", "orient"), None),
        P(("dom", "orient"), None),
        P(("dom", "orient"), None),
    )
    out_specs = (P(("dom", "orient"), "cls"), P(None, "cls", "orient", "dom"))
    return jax.shard_map(local, mesh=mesh, in_specs=in_specs, out_specs=out_specs, check_vma=False)
```

```python
import functools
import math

import jax
import jax.numpy as jnp
import numpy as np
from jax import lax
from jax.experimental import pallas as pl
from jax.experimental.pallas import tpu as pltpu
from jax.sharding import PartitionSpec as P

IMG = 256
TX = 8
TY = 8
MESH = pl.DeviceIdType.MESH
F32 = jnp.float32
BF16 = jnp.bfloat16


def kernel(
    doms, zs, refs, imgs, xcos, xsin, ycos, ysin, oid, sid, fixed, prob_out, vol_out,
    ref_all, sib, out_rows, in_rows, xs, rs, acc, got, stat, stat_in, mix, mix_in, slab, slab_in,
    plane_s, plane_r, sib_s, sib_r, row_s, row_r, ring_s, ring_r, one_s, one_r, mix_s, mix_r, z_s, z_r,
):
    here = imgs.shape[1]
    band = imgs.shape[2] // doms
    lines = band // IMG
    half = doms // 2
    columns = refs.shape[1]
    classes = columns // zs
    me_d, me_z, me_c = lax.axis_index("dom"), lax.axis_index("orient"), lax.axis_index("cls")
    core, me_q = me_d % 2, me_d // 2
    twin = me_d + 1 - 2 * core
    other = 1 - me_c

    def send(src, dst, s, r, to):
        return pltpu.make_async_remote_copy(
            src_ref=src, dst_ref=dst, send_sem=s, recv_sem=r, device_id=to, device_id_type=MESH
        )

    barrier = pltpu.get_barrier_semaphore()

    @pl.loop(1, doms)
    def _(i):
        pl.semaphore_signal(barrier, inc=1, device_id={"dom": (me_d + i) % doms}, device_id_type=MESH)

    @pl.loop(1, zs)
    def _(i):
        pl.semaphore_signal(barrier, inc=1, device_id={"orient": (me_z + i) % zs}, device_id_type=MESH)

    pl.semaphore_signal(barrier, inc=1, device_id={"cls": other}, device_id_type=MESH)
    pl.semaphore_wait(barrier, doms + zs - 1)

    def plane_copy(i):
        return send(
            refs, ref_all.at[me_z, me_q], plane_s.at[i], plane_r.at[i],
            {"dom": 2 * ((me_q + i) % half) + core},
        )

    @pl.loop(1, half)
    def _(i):
        plane_copy(i).start()

    ref_all[me_z, me_q] = refs[...]

    def sib_copy(q):
        start = pl.multiple_of((2 * q + 1 - core) * band, band)
        return send(imgs.at[:, :, pl.ds(start, band)], sib.at[q], sib_s.at[q], sib_r.at[q], {"dom": twin})

    @pl.loop(0, half)
    def _(q):
        sib_copy(q).start()

    def row_copy(i):
        return send(
            out_rows.at[i], in_rows.at[:, me_d], row_s.at[i], row_r.at[i], {"dom": (me_d + i) % doms}
        )

    shift = jnp.broadcast_to(sid[...], (here, 128))
    at_x, at_y = shift & (TX - 1), shift >> 3
    twice = lambda v: jnp.concatenate([v, v], axis=1)
    wide_x = twice(at_x)
    px_c = jnp.zeros((here, IMG), F32)
    px_s = jnp.zeros((here, IMG), F32)
    for a in range(TX):
        px_c = jnp.where(wide_x == a, xcos[a : a + 1, :], px_c)
        px_s = jnp.where(wide_x == a, xsin[a : a + 1, :], px_s)

    @pl.loop(0, doms)
    def _(i):
        d = (me_d + i) % doms

        @pl.loop(0, lines)
        def _(r):
            col = pl.multiple_of(d * band + r * IMG, IMG)
            re = imgs[0, :, pl.ds(col, IMG)].astype(F32)
            im = imgs[1, :, pl.ds(col, IMG)].astype(F32)
            py_c = jnp.zeros((here, 128), F32)
            py_s = jnp.zeros((here, 128), F32)
            for b in range(TY):
                py_c = jnp.where(at_y == b, ycos[(d * lines + r) * TY + b], py_c)
                py_s = jnp.where(at_y == b, ysin[(d * lines + r) * TY + b], py_s)
            py_c, py_s = twice(py_c), twice(py_s)
            c = px_c * py_c - px_s * py_s
            s = px_s * py_c + px_c * py_s
            to = pl.ds(pl.multiple_of(r * IMG, IMG), IMG)
            out_rows[i, 0, :, to] = (re * c - im * s).astype(BF16)
            out_rows[i, 1, :, to] = (re * s + im * c).astype(BF16)

        @pl.when(i > 0)
        def _():
            row_copy(i).start()

    in_rows[:, me_d] = out_rows[0]

    acc[...] = jnp.zeros_like(acc)

    @pl.loop(1, half)
    def _(i):
        plane_copy(i).wait()

    low, high = pl.ds(0, half // 2), pl.ds(half // 2, half // 2)
    right, left = (me_z + 1) % zs, (me_z + zs - 1) % zs

    def ring_copy(way, s, part):
        block = (me_z + zs - s) % zs if way == 0 else (me_z + s) % zs
        at = ref_all.at[block, low if part == 0 else high]
        n = 2 * way + part
        return send(at, at, ring_s.at[n, s], ring_r.at[n, s], {"orient": right if way == 0 else left})

    def correlate(block, q):
        d = 2 * q + core
        col = pl.multiple_of(d * band + block * IMG, IMG)
        near = pl.ds(pl.multiple_of(block * IMG, IMG), IMG)
        for n in range(2):
            if n == 0:
                re, im = imgs[0, :, pl.ds(col, IMG)], imgs[1, :, pl.ds(col, IMG)]
            else:
                re, im = sib[q, 0, :, near], sib[q, 1, :, near]
            row = n * TX * here
            mid = row + TX // 2 * here
            xs[mid : mid + here, 0:IMG] = re
            xs[mid : mid + here, IMG:] = im
            re, im = re.astype(F32), im.astype(F32)
            for t in range(1, TX // 2 + 1):
                a = TX // 2 - t
                co, si = xcos[a : a + 1, :], xsin[a : a + 1, :]
                rc, rsn, ic, isn = re * co, re * si, im * co, im * si
                at = row + a * here
                xs[at : at + here, 0:IMG] = (rc - isn).astype(BF16)
                xs[at : at + here, IMG:] = (rsn + ic).astype(BF16)
                if t < TX // 2:
                    at = row + (TX // 2 + t) * here
                    xs[at : at + here, 0:IMG] = (rc + isn).astype(BF16)
                    xs[at : at + here, IMG:] = (ic - rsn).astype(BF16)
        re, im = ref_all[block, q, 0], ref_all[block, q, 1]
        mid = TY // 2 * columns
        rs[mid : mid + columns, 0:IMG] = re
        rs[mid : mid + columns, IMG:] = im
        re, im = re.astype(F32), im.astype(F32)
        ky = (d * lines + block) * TY
        for t in range(1, TY // 2 + 1):
            b = TY // 2 - t
            co, si = ycos[ky + b], ysin[ky + b]
            rc, rsn, ic, isn = re * co, re * si, im * co, im * si
            at = b * columns
            rs[at : at + columns, 0:IMG] = (rc + isn).astype(BF16)
            rs[at : at + columns, IMG:] = (ic - rsn).astype(BF16)
            if t < TY // 2:
                at = (TY // 2 + t) * columns
                rs[at : at + columns, 0:IMG] = (rc - isn).astype(BF16)
                rs[at : at + columns, IMG:] = (ic + rsn).astype(BF16)
        acc[...] += lax.dot_general(
            xs[...], rs[...], (((1,), (1,)), ((), ())), preferred_element_type=F32
        )

    @pl.loop(0, half)
    def _(q):
        sib_copy(q).wait()

    steps = zs // 2

    @pl.loop(0, steps + 1)
    def _(s):
        @pl.when(s < steps)
        def _():
            ring_copy(0, s, 0).start()
            ring_copy(1, s, 1).start()

        @pl.when(s < steps - 1)
        def _():
            ring_copy(0, s, 1).start()
            ring_copy(1, s, 0).start()

        blocks = jnp.where((s == 0) | (s == steps), half, 2 * half)

        @pl.loop(0, blocks)
        def _(j):
            block = jnp.where(j < half, me_z + zs - s, me_z + s) % zs
            correlate(block, j % half)

        @pl.when(s < steps)
        def _():
            ring_copy(0, s, 0).wait()
            ring_copy(1, s, 1).wait()

        @pl.when(s < steps - 1)
        def _():
            ring_copy(0, s, 1).wait()
            ring_copy(1, s, 0).wait()

    rows = TX * here
    swap = send(acc.at[pl.ds(rows, rows)], got, one_s.at[0], one_r.at[0], {"dom": twin})
    swap.start()
    swap.wait()
    logits = (acc[0:rows] + got[...]).reshape(TX, here, TY * columns)
    top = jnp.max(jnp.max(logits, axis=0), axis=1, keepdims=True)
    grown = jnp.sum(jnp.exp(logits - top[None]), axis=0)
    lane = lax.broadcasted_iota(jnp.int32, (here, TY * columns), 1)
    of_class = (lane // zs) % classes
    sums = [jnp.sum(jnp.where(of_class == k, grown, 0.0), axis=1, keepdims=True) for k in range(classes)]
    total = sums[0]
    for k in range(1, classes):
        total = total + sums[k]
    lane = lax.broadcasted_iota(jnp.int32, (here, 128), 1)
    stat[...] = jnp.where(lane == 0, top, total)
    pair = send(stat, stat_in, one_s.at[1], one_r.at[1], {"cls": other})
    pair.start()
    pair.wait()
    top_in, total_in = stat_in[:, 0:1], stat_in[:, 1:2]
    both = jnp.maximum(top, top_in)
    scale = jnp.exp(top - both)
    total = total * scale + total_in * jnp.exp(top_in - both)
    probs = [sums[k] * scale / total for k in range(classes)]

    value = jnp.zeros((here, 128), F32)
    for k in range(classes):
        prob_out[:, k : k + 1] = probs[k]
        value = jnp.where(lane % classes == k, (fixed[...] * probs[k]).astype(BF16).astype(F32), value)
    wide = 2 * classes
    hit = ((lane // classes) % 2 == lane // (wide * zs)) & ((lane // wide) % zs == oid[...])
    mix[...] = jnp.where(hit, value, 0.0).astype(BF16)

    def mix_copy(i):
        return send(mix, mix_in.at[me_d], mix_s.at[i], mix_r.at[i], {"dom": (me_d + i) % doms})

    @pl.loop(1, doms)
    def _(i):
        mix_copy(i).start()

    mix_in[me_d] = mix[...]

    @pl.loop(1, doms)
    def _(i):
        row_copy(i).wait()

    @pl.loop(1, doms)
    def _(i):
        mix_copy(i).wait()

    turned = mix_in[...].reshape(doms * here, 128).astype(F32).T.astype(BF16)
    count = wide * zs
    part = jnp.dot(
        turned[0:count], in_rows[0].reshape(doms * here, band), preferred_element_type=F32
    ) + jnp.dot(turned[count:], in_rows[1].reshape(doms * here, band), preferred_element_type=F32)
    for o in range(zs):
        slab[o] = part[o * wide : (o + 1) * wide].astype(BF16)

    def z_copy(i):
        return send(slab.at[(me_z + i) % zs], slab_in.at[i], z_s.at[i], z_r.at[i], {"orient": (me_z + i) % zs})

    @pl.loop(1, zs)
    def _(i):
        z_copy(i).start()

    slab_in[0] = slab[me_z]

    @pl.loop(1, zs)
    def _(i):
        z_copy(i).wait()

    out = slab_in[0].astype(F32)
    for i in range(1, zs):
        out = out + slab_in[i].astype(F32)
    vol_out[...] = out


def tables():
    kx = np.arange(IMG) - IMG // 2
    ky = np.arange(IMG // 2)
    turn_x = 2 * np.pi / IMG * ((np.arange(TX) - TX // 2)[:, None] * kx[None, :])
    turn_y = 2 * np.pi / IMG * (ky[:, None] * (np.arange(TY) - TY // 2)[None, :])
    return [
        f(t).astype(np.float32) for t in (turn_x, turn_y.reshape(-1)) for f in (np.cos, np.sin)
    ]


def solution(mesh):
    doms, zs = mesh.shape["dom"], mesh.shape["orient"]

    def local(references, images, orient_lists, shift_ids, fixed_weights):
        classes, here = references.shape[1], images.shape[1]
        columns = classes * references.shape[2]
        band = images.shape[2] // doms
        half = doms // 2
        vmem, smem = pl.BlockSpec(memory_space=pltpu.VMEM), pl.BlockSpec(memory_space=pltpu.SMEM)
        dma = pltpu.SemaphoreType.DMA
        rows = TX * here
        prob, volume = pl.pallas_call(
            functools.partial(kernel, doms, zs),
            out_shape=(
                jax.ShapeDtypeStruct((here, classes), F32),
                jax.ShapeDtypeStruct((2 * classes, band), F32),
            ),
            in_specs=[vmem] * 4 + [smem] * 2 + [vmem] * 3,
            out_specs=(vmem, vmem),
            scratch_shapes=[
                pltpu.VMEM((zs, half, 2, columns, IMG), BF16),
                pltpu.VMEM((half, 2, here, band), BF16),
                pltpu.VMEM((doms, 2, here, band), BF16),
                pltpu.VMEM((2, doms, here, band), BF16),
                pltpu.VMEM((2 * rows, 2 * IMG), BF16),
                pltpu.VMEM((TY * columns, 2 * IMG), BF16),
                pltpu.VMEM((2 * rows, TY * columns), F32),
                pltpu.VMEM((rows, TY * columns), F32),
                pltpu.VMEM((here, 128), F32),
                pltpu.VMEM((here, 128), F32),
                pltpu.VMEM((here, 128), BF16),
                pltpu.VMEM((doms, here, 128), BF16),
                pltpu.VMEM((zs, 2 * classes, band), BF16),
                pltpu.VMEM((zs, 2 * classes, band), BF16),
                dma((half,)), dma((half,)),
                dma((half,)), dma((half,)),
                dma((doms,)), dma((doms,)),
                dma((4, zs // 2)), dma((4, zs // 2)),
                dma((2,)), dma((2,)),
                dma((doms,)), dma((doms,)),
                dma((zs,)), dma((zs,)),
            ],
            compiler_params=pltpu.CompilerParams(
                collective_id=0, has_side_effects=True, vmem_limit_bytes=40 << 20
            ),
            name="estep",
        )(
            references.reshape(2, columns, references.shape[3]),
            images,
            *[jnp.asarray(t) for t in tables()],
            orient_lists,
            shift_ids,
            fixed_weights,
        )
        return prob, volume.reshape(2, classes, 1, band)

    in_specs = (
        P(None, "cls", None, ("dom", "orient")),
        P(None, ("dom", "orient"), None),
        P(("dom", "orient"), None),
        P(("dom", "orient"), None),
        P(("dom", "orient"), None),
    )
    out_specs = (P(("dom", "orient"), "cls"), P(None, "cls", "orient", "dom"))
    return jax.shard_map(local, mesh=mesh, in_specs=in_specs, out_specs=out_specs, check_vma=False)
```

```python
import functools
import math

import jax
import jax.numpy as jnp
import numpy as np
from jax import lax
from jax.experimental import pallas as pl
from jax.experimental.pallas import tpu as pltpu
from jax.sharding import PartitionSpec as P

IMG = 256
TX = 8
TY = 8
MESH = pl.DeviceIdType.MESH
F32 = jnp.float32
BF16 = jnp.bfloat16


def kernel(
    doms, zs, refs, images, xtab_in, ytab_in, oid_in, sid_in, fixed_in, prob_out, vol_out,
    imgs, xtab, ytab, oid_row, sid_row, fixed_row,
    ref_all, sib, out_rows, in_rows, xs_a, rs_a, xs_b, rs_b, acc, got, stat, pair_in, mix, mix_in, slab, slab_in,
    plane_s, plane_r, sib_s, sib_r, row_s, row_r, ring_s, ring_r, one_s, one_r, mix_s, mix_r, z_s, z_r, in_s,
):
    here = images.shape[1]
    band = images.shape[2] // doms
    lines = band // IMG
    half = doms // 2
    side = half // 2
    columns = refs.shape[1]
    classes = columns // zs
    steps = zs // 2
    me_d, me_z, me_c = lax.axis_index("dom"), lax.axis_index("orient"), lax.axis_index("cls")
    core, me_q = me_d % 2, me_d // 2
    me_x, me_l = me_q % side, me_q // side
    me_y = 2 * me_c + me_l
    twin = me_d + 1 - 2 * core
    other = 1 - me_c

    def send(src, dst, s, r, to):
        return pltpu.make_async_remote_copy(
            src_ref=src, dst_ref=dst, send_sem=s, recv_sem=r, device_id=to, device_id_type=MESH
        )

    barrier = pltpu.get_barrier_semaphore()

    def greet(to):
        pl.semaphore_signal(barrier, inc=1, device_id=to, device_id_type=MESH)

    @pl.loop(1, doms)
    def _(i):
        greet({"dom": (me_d + i) % doms})

    @pl.loop(1, zs)
    def _(i):
        greet({"orient": (me_z + i) % zs})

    greet({"cls": other})

    @pl.loop(0, half)
    def _(i):
        greet({"dom": half * (1 - me_l) + i, "cls": other})

    loads = [
        pltpu.make_async_copy(src, dst, in_s.at[n])
        for n, (src, dst) in enumerate(
            (
                (refs, ref_all.at[me_z, me_q]),
                (images, imgs),
                (xtab_in, xtab),
                (ytab_in, ytab),
                (oid_in, oid_row),
                (sid_in, sid_row),
                (fixed_in, fixed_row),
            )
        )
    ]
    for load in loads:
        load.start()
    pl.semaphore_wait(barrier, doms + zs - 1 + half)

    def plane_copy(j):
        to = (me_l + j // side) % 2 * side + (me_x + j % side) % side
        at = ref_all.at[me_z, me_q]
        return send(at, at, plane_s.at[j], plane_r.at[j], {"dom": 2 * to + core})

    def piece(j):
        return (me_l + j // side) % 2 * side + (me_x + side - j % side) % side

    def sib_copy(q):
        start = pl.multiple_of((2 * q + 1 - core) * band, band)
        return send(images.at[:, :, pl.ds(start, band)], sib.at[q], sib_s.at[q], sib_r.at[q], {"dom": twin})

    right, left = (me_z + 1) % zs, (me_z + zs - 1) % zs

    def ring_copy(way, s, j):
        block = (me_z + zs + 1 - s) % zs if way == 0 else (me_z + s - 1) % zs
        at = ref_all.at[block, piece(j)]
        return send(
            at, at, ring_s.at[way, s - 1, j], ring_r.at[way, s - 1, j], {"orient": right if way == 0 else left}
        )

    loads[0].wait()
    ring_copy(0, 1, 0).start()
    ring_copy(1, 1, 0).start()

    @pl.loop(1, half)
    def _(j):
        plane_copy(j).start()

    @pl.loop(0, half)
    def _(q):
        sib_copy(q).start()

    for load in loads[1:]:
        load.wait()

    xcos, xsin = xtab.at[0], xtab.at[1]
    ycos, ysin = (lambda n: ytab[0, n]), (lambda n: ytab[1, n])
    diagonal = lax.broadcasted_iota(jnp.int32, (here, here), 0) == lax.broadcasted_iota(
        jnp.int32, (here, here), 1
    )

    def column(row):
        wide = jnp.broadcast_to(row[...].astype(F32), (here, here))
        return jnp.sum(jnp.where(diagonal, wide, 0.0), axis=1, keepdims=True)

    oid, sid, fixed = column(oid_row).astype(jnp.int32), column(sid_row).astype(jnp.int32), column(fixed_row)
    shift = jnp.broadcast_to(sid, (here, 128))
    at_x, at_y = shift & (TX - 1), shift >> 3
    twice = lambda v: jnp.concatenate([v, v], axis=1)
    wide_x = twice(at_x)
    px_c = jnp.zeros((here, IMG), F32)
    px_s = jnp.zeros((here, IMG), F32)
    for a in range(TX):
        px_c = jnp.where(wide_x == a, xcos[a : a + 1, :], px_c)
        px_s = jnp.where(wide_x == a, xsin[a : a + 1, :], px_s)

    def band_of(i):
        return 2 * ((me_l + i // half) % 2 * side + (me_x + i // 2 % side) % side) + (core + i % 2) % 2

    def row_copy(i):
        return send(out_rows.at[i], in_rows.at[:, me_d], row_s.at[i], row_r.at[i], {"dom": band_of(i)})

    def part_copy(i, r):
        n = i + r * half
        y = (me_y + (1 if r == 0 else 3)) % 4
        return send(
            out_rows.at[i, r], in_rows.at[r, me_d], row_s.at[n], row_r.at[n], {"dom": band_of(i), "cls": y // 2}
        )

    @pl.loop(0, doms)
    def _(i):
        d = band_of(i)

        @pl.loop(0, lines)
        def _(r):
            col = pl.multiple_of(d * band + r * IMG, IMG)
            re = imgs[0, :, pl.ds(col, IMG)].astype(F32)
            im = imgs[1, :, pl.ds(col, IMG)].astype(F32)
            py_c = jnp.zeros((here, 128), F32)
            py_s = jnp.zeros((here, 128), F32)
            for b in range(TY):
                py_c = jnp.where(at_y == b, ycos((d * lines + r) * TY + b), py_c)
                py_s = jnp.where(at_y == b, ysin((d * lines + r) * TY + b), py_s)
            py_c, py_s = twice(py_c), twice(py_s)
            c = px_c * py_c - px_s * py_s
            s = px_s * py_c + px_c * py_s
            to = pl.ds(pl.multiple_of(r * IMG, IMG), IMG)
            out_rows[i, 0, :, to] = (re * c - im * s).astype(BF16)
            out_rows[i, 1, :, to] = (re * s + im * c).astype(BF16)

        @pl.when((i > 0) & (i < half))
        def _():
            row_copy(i).start()

        @pl.when(i >= half)
        def _():
            part_copy(i, 0).start()
            part_copy(i, 1).start()

    in_rows[:, me_d] = out_rows[0]

    acc[...] = jnp.zeros_like(acc)
    xs_b[...] = jnp.zeros_like(xs_b)
    rs_b[...] = jnp.zeros_like(rs_b)

    def prepare(xs, rs, block, q):
        d = 2 * q + core
        col = pl.multiple_of(d * band + block * IMG, IMG)
        near = pl.ds(pl.multiple_of(block * IMG, IMG), IMG)
        for n in range(2):
            if n == 0:
                re, im = imgs[0, :, pl.ds(col, IMG)], imgs[1, :, pl.ds(col, IMG)]
            else:
                re, im = sib[q, 0, :, near], sib[q, 1, :, near]
            row = n * TX * here
            mid = row + TX // 2 * here
            xs[mid : mid + here, 0:IMG] = re
            xs[mid : mid + here, IMG:] = im
            re, im = re.astype(F32), im.astype(F32)
            for t in range(1, TX // 2 + 1):
                a = TX // 2 - t
                co, si = xcos[a : a + 1, :], xsin[a : a + 1, :]
                rc, rsn, ic, isn = re * co, re * si, im * co, im * si
                at = row + a * here
                xs[at : at + here, 0:IMG] = (rc - isn).astype(BF16)
                xs[at : at + here, IMG:] = (rsn + ic).astype(BF16)
                if t < TX // 2:
                    at = row + (TX // 2 + t) * here
                    xs[at : at + here, 0:IMG] = (rc + isn).astype(BF16)
                    xs[at : at + here, IMG:] = (ic - rsn).astype(BF16)
        re, im = ref_all[block, q, 0], ref_all[block, q, 1]
        mid = TY // 2 * columns
        rs[mid : mid + columns, 0:IMG] = re
        rs[mid : mid + columns, IMG:] = im
        re, im = re.astype(F32), im.astype(F32)
        ky = (d * lines + block) * TY
        for t in range(1, TY // 2 + 1):
            b = TY // 2 - t
            co, si = ycos(ky + b), ysin(ky + b)
            rc, rsn, ic, isn = re * co, re * si, im * co, im * si
            at = b * columns
            rs[at : at + columns, 0:IMG] = (rc + isn).astype(BF16)
            rs[at : at + columns, IMG:] = (ic - rsn).astype(BF16)
            if t < TY // 2:
                at = (TY // 2 + t) * columns
                rs[at : at + columns, 0:IMG] = (rc - isn).astype(BF16)
                rs[at : at + columns, IMG:] = (ic + rsn).astype(BF16)

    def add(xs, rs):
        acc[...] += lax.dot_general(
            xs[...], rs[...], (((1,), (1,)), ((), ())), preferred_element_type=F32
        )

    @pl.loop(0, half)
    def _(q):
        sib_copy(q).wait()

    first, middle = half // 2, half * (steps - 1)

    @pl.loop(0, half + middle)
    def _(t):
        @pl.when(t < first)
        def _():
            for n in range(2):
                j = 2 * t + n

                @pl.when(j > 0)
                def _():
                    plane_copy(j).wait_recv()
                    ring_copy(0, 1, j).start()
                    ring_copy(1, 1, j).start()

        @pl.when((t >= first) & (t < first + middle))
        def _():
            s, j = 1 + (t - first) // half, (t - first) % half
            ring_copy(0, s, j).wait_recv()

            @pl.when((s < steps - 1) | (j < half // 2))
            def _():
                ring_copy(0, s + 1, j).start()

            ring_copy(1, s, j).wait_recv()

            @pl.when((s < steps - 1) | (j >= half // 2))
            def _():
                ring_copy(1, s + 1, j).start()

        @pl.when(t >= first + middle)
        def _():
            j = t - first - middle
            ring_copy(0, steps, j).wait_recv()
            ring_copy(1, steps, j + half // 2).wait_recv()

        at_first, at_last = t < first, t >= first + middle
        s, j = 1 + (t - first) // half, (t - first) % half
        near = jnp.where(at_last, steps, jnp.where(at_first, 0, s))
        j_a = jnp.where(at_last, t - first - middle, jnp.where(at_first, 2 * t, j))
        j_b = jnp.where(at_last, j_a + half // 2, jnp.where(at_first, 2 * t + 1, j))
        prepare(xs_a, rs_a, (me_z + zs - near) % zs, piece(j_a))
        add(xs_b, rs_b)
        prepare(xs_b, rs_b, (me_z + near) % zs, piece(j_b))
        add(xs_a, rs_a)

    add(xs_b, rs_b)

    rows = TX * here
    swap = send(acc.at[pl.ds(rows, rows)], got, one_s.at[0], one_r.at[0], {"dom": twin})
    swap.start()
    swap.wait()
    logits = (acc[0:rows] + got[...]).reshape(TX, here, TY * columns)
    top = jnp.max(jnp.max(logits, axis=0), axis=1, keepdims=True)
    grown = jnp.sum(jnp.exp(logits - top[None]), axis=0)
    lane = lax.broadcasted_iota(jnp.int32, (here, TY * columns), 1)
    of_class = (lane // zs) % classes
    sums = [jnp.sum(jnp.where(of_class == k, grown, 0.0), axis=1, keepdims=True) for k in range(classes)]
    total = sums[0]
    for k in range(1, classes):
        total = total + sums[k]

    lane = lax.broadcasted_iota(jnp.int32, (here, 128), 1)
    fields = jnp.zeros((here, 128), F32)
    for n, v in enumerate((*sums, top, total, fixed, oid.astype(F32))):
        fields = jnp.where(lane == n, v, fields)
    fields = jnp.concatenate([fields, jnp.zeros((128 - here, 128), F32)], axis=0).T
    stat[...] = fields[0 : 2 * classes]
    pair = send(stat, pair_in, one_s.at[1], one_r.at[1], {"cls": other})
    pair.start()
    pair.wait()
    mine, theirs = stat[...], pair_in[...]
    top_a, top_b = mine[classes : classes + 1], theirs[classes : classes + 1]
    both = jnp.maximum(top_a, top_b)
    scale = jnp.exp(top_a - both)
    total = mine[classes + 1 : classes + 2] * scale + theirs[classes + 1 : classes + 2] * jnp.exp(top_b - both)
    prob = mine[0:classes] * scale / total
    prob_out[...] = prob[:, 0:here]
    weight = (mine[classes + 2 : classes + 3] * prob).astype(BF16).astype(F32)
    tile = jnp.concatenate([weight, mine[2 * classes - 1 :], jnp.zeros((classes - 1, 128), F32)], axis=0)
    tile = jnp.where(lax.broadcasted_iota(jnp.int32, tile.shape, 1) < here, tile, 0.0)
    packs = 128 // here
    mix[...] = pltpu.roll(tile, me_d % packs * here, 1)

    def mix_copy(i):
        return send(mix, mix_in.at[me_d], mix_s.at[i], mix_r.at[i], {"dom": (me_d + i) % doms})

    @pl.loop(1, doms)
    def _(i):
        mix_copy(i).start()

    mix_in[me_d] = mix[...]

    @pl.loop(1, half)
    def _(i):
        row_copy(i).wait()

    @pl.loop(half, doms)
    def _(i):
        part_copy(i, 0).wait()
        part_copy(i, 1).wait()

    @pl.loop(1, doms)
    def _(i):
        mix_copy(i).wait()

    got_mix = [jnp.sum(mix_in[n : n + packs], axis=0) for n in range(0, doms, packs)]
    got_mix = jnp.concatenate(got_mix, axis=1)
    wide = 2 * classes
    of_entry = jnp.broadcast_to(got_mix[classes : classes + 1].astype(jnp.int32), (wide, doms * here))
    weight = got_mix[0:classes]
    none = jnp.zeros_like(weight)

    def grow(part):
        rows = jnp.concatenate([weight, none] if part == 0 else [none, weight], axis=0)
        mixing = jnp.concatenate([jnp.where(of_entry == o, rows, 0.0) for o in range(zs)], axis=0)
        return jnp.dot(
            mixing.astype(BF16), in_rows[part].reshape(doms * here, band), preferred_element_type=F32
        )

    volume = grow(0) + grow(1)
    for o in range(zs):
        slab[o] = volume[o * wide : (o + 1) * wide].astype(BF16)

    def z_copy(i):
        return send(slab.at[(me_z + i) % zs], slab_in.at[i], z_s.at[i], z_r.at[i], {"orient": (me_z + i) % zs})

    for i in sorted(range(1, zs), key=lambda i: -min(i, zs - i)):
        z_copy(i).start()

    slab_in[0] = slab[me_z]

    @pl.loop(1, half)
    def _(j):
        plane_copy(j).wait_send()

    @pl.loop(0, steps * half)
    def _(n):
        s, j = 1 + n // half, n % half

        @pl.when((s < steps) | (j < half // 2))
        def _():
            ring_copy(0, s, j).wait_send()

        @pl.when((s < steps) | (j >= half // 2))
        def _():
            ring_copy(1, s, j).wait_send()

    @pl.loop(1, zs)
    def _(i):
        z_copy(i).wait()

    out = slab_in[0].astype(F32)
    for i in range(1, zs):
        out = out + slab_in[i].astype(F32)
    vol_out[...] = out


def tables():
    kx = np.arange(IMG) - IMG // 2
    ky = np.arange(IMG // 2)
    turn_x = 2 * np.pi / IMG * ((np.arange(TX) - TX // 2)[:, None] * kx[None, :])
    turn_y = 2 * np.pi / IMG * (ky[:, None] * (np.arange(TY) - TY // 2)[None, :])
    return [
        np.stack([np.cos(t), np.sin(t)]).astype(np.float32) for t in (turn_x, turn_y.reshape(-1))
    ]


def solution(mesh):
    doms, zs = mesh.shape["dom"], mesh.shape["orient"]

    def local(references, images, orient_lists, shift_ids, fixed_weights):
        classes, here = references.shape[1], images.shape[1]
        columns = classes * references.shape[2]
        band = images.shape[2] // doms
        half = doms // 2
        vmem, hbm = pl.BlockSpec(memory_space=pltpu.VMEM), pl.BlockSpec(memory_space=pltpu.MemorySpace.HBM)
        dma = pltpu.SemaphoreType.DMA
        rows = TX * here
        prob, volume = pl.pallas_call(
            functools.partial(kernel, doms, zs),
            out_shape=(
                jax.ShapeDtypeStruct((classes, here), F32),
                jax.ShapeDtypeStruct((2 * classes, band), F32),
            ),
            in_specs=[hbm] * 7,
            out_specs=(vmem, vmem),
            scratch_shapes=[
                pltpu.VMEM((2, here, images.shape[2]), BF16),
                pltpu.VMEM((2, TX, IMG), F32),
                pltpu.SMEM((2, IMG // 2 * TY), F32),
                pltpu.VMEM((1, here), jnp.int32),
                pltpu.VMEM((1, here), jnp.int32),
                pltpu.VMEM((1, here), F32),
                pltpu.VMEM((zs, half, 2, columns, IMG), BF16),
                pltpu.VMEM((half, 2, here, band), BF16),
                pltpu.VMEM((doms, 2, here, band), BF16),
                pltpu.VMEM((2, doms, here, band), BF16),
                pltpu.VMEM((2 * rows, 2 * IMG), BF16),
                pltpu.VMEM((TY * columns, 2 * IMG), BF16),
                pltpu.VMEM((2 * rows, 2 * IMG), BF16),
                pltpu.VMEM((TY * columns, 2 * IMG), BF16),
                pltpu.VMEM((2 * rows, TY * columns), F32),
                pltpu.VMEM((rows, TY * columns), F32),
                pltpu.VMEM((2 * classes, 128), F32),
                pltpu.VMEM((2 * classes, 128), F32),
                pltpu.VMEM((2 * classes, 128), F32),
                pltpu.VMEM((doms, 2 * classes, 128), F32),
                pltpu.VMEM((zs, 2 * classes, band), BF16),
                pltpu.VMEM((zs, 2 * classes, band), BF16),
                dma((half,)), dma((half,)),
                dma((half,)), dma((half,)),
                dma((doms + half,)), dma((doms + half,)),
                dma((2, zs // 2, half)), dma((2, zs // 2, half)),
                dma((2,)), dma((2,)),
                dma((doms,)), dma((doms,)),
                dma((zs,)), dma((zs,)),
                dma((7,)),
            ],
            compiler_params=pltpu.CompilerParams(
                collective_id=0, has_side_effects=True, vmem_limit_bytes=48 << 20
            ),
            name="estep",
        )(
            *[
                pltpu.with_memory_space_constraint(v, pltpu.MemorySpace.HBM)
                for v in (
                    references.reshape(2, columns, references.shape[3]),
                    images,
                    *[jnp.asarray(t) for t in tables()],
                    orient_lists.reshape(1, here),
                    shift_ids.reshape(1, here),
                    fixed_weights.reshape(1, here),
                )
            ]
        )
        return prob.T, volume.reshape(2, classes, 1, band)

    in_specs = (
        P(None, "cls", None, ("dom", "orient")),
        P(None, ("dom", "orient"), None),
        P(("dom", "orient"), None),
        P(("dom", "orient"), None),
        P(("dom", "orient"), None),
    )
    out_specs = (P(("dom", "orient"), "cls"), P(None, "cls", "orient", "dom"))
    return jax.shard_map(local, mesh=mesh, in_specs=in_specs, out_specs=out_specs, check_vma=False)
```

```python
import functools
import math

import jax
import jax.numpy as jnp
import numpy as np
from jax import lax
from jax.experimental import pallas as pl
from jax.experimental.pallas import tpu as pltpu
from jax.sharding import PartitionSpec as P

IMG = 256
TX = 8
TY = 8
MESH = pl.DeviceIdType.MESH
NEAR_ROWS = 12
F32 = jnp.float32
BF16 = jnp.bfloat16


def kernel(
    doms, zs, refs, images, xtab_in, ytab_in, oid_in, sid_in, fixed_in, prob_out, vol_out,
    imgs, xtab, ytab, oid_row, sid_row, fixed_row,
    ref_all, sib, out_rows, in_rows, xs_a, rs_a, xs_b, rs_b, acc, got, stat, stat_in, slab, slab_in,
    plane_s, plane_r, sib_s, sib_r, row_s, row_r, ring_s, ring_r, one_s, one_r, mix_s, mix_r, z_s, z_r, in_s,
):
    here = images.shape[1]
    band = images.shape[2] // doms
    lines = band // IMG
    half = doms // 2
    side = half // 2
    columns = refs.shape[1]
    classes = columns // zs
    steps = zs // 2
    me_d, me_z, me_c = lax.axis_index("dom"), lax.axis_index("orient"), lax.axis_index("cls")
    core, me_q = lax.rem(me_d, 2), lax.div(me_d, 2)
    me_x, me_l = lax.rem(me_q, side), lax.div(me_q, side)
    twin = me_d + 1 - 2 * core

    def wrap(v, n):
        return jnp.where(v >= n, v - n, v)

    other = 1 - me_c

    def send(src, dst, s, r, to):
        return pltpu.make_async_remote_copy(
            src_ref=src, dst_ref=dst, send_sem=s, recv_sem=r, device_id=to, device_id_type=MESH
        )

    barrier = pltpu.get_barrier_semaphore()

    def greet(to):
        pl.semaphore_signal(barrier, inc=1, device_id=to, device_id_type=MESH)

    @pl.loop(1, doms)
    def _(i):
        greet({"dom": wrap(me_d + i, doms)})

    @pl.loop(1, zs)
    def _(i):
        greet({"orient": wrap(me_z + i, zs)})

    @pl.loop(0, doms)
    def _(i):
        greet({"dom": i, "cls": other})

    loads = [
        pltpu.make_async_copy(src, dst, in_s.at[n])
        for n, (src, dst) in enumerate(
            (
                (refs, ref_all.at[me_z, me_q]),
                (images, imgs),
                (xtab_in, xtab),
                (ytab_in, ytab),
                (oid_in, oid_row),
                (sid_in, sid_row),
                (fixed_in, fixed_row),
            )
        )
    ]
    for load in loads:
        load.start()
    pl.semaphore_wait(barrier, 2 * doms + zs - 2)

    def plane_copy(j):
        low = wrap(j, side)
        to = jnp.where(j < side, me_l, 1 - me_l) * side + wrap(me_x + low, side)
        at = ref_all.at[me_z, me_q]
        return send(at, at, plane_s.at[j], plane_r.at[j], {"dom": 2 * to + core})

    def piece(j):
        low = wrap(j, side)
        return jnp.where(j < side, me_l, 1 - me_l) * side + wrap(me_x + side - low, side)

    def sib_copy(q):
        start = pl.multiple_of((2 * q + 1 - core) * band, band)
        return send(images.at[:, :, pl.ds(start, band)], sib.at[q], sib_s.at[q], sib_r.at[q], {"dom": twin})

    right, left = wrap(me_z + 1, zs), wrap(me_z + zs - 1, zs)

    def ring_copy(way, s, j):
        block = wrap(me_z + zs + 1 - s, zs) if way == 0 else wrap(me_z + s - 1, zs)
        at = ref_all.at[block, piece(j)]
        return send(
            at, at, ring_s.at[way, s - 1, j], ring_r.at[way, s - 1, j], {"orient": right if way == 0 else left}
        )

    loads[0].wait()
    ring_copy(0, 1, 0).start()
    ring_copy(1, 1, 0).start()

    @pl.loop(1, half)
    def _(j):
        plane_copy(j).start()

    @pl.loop(0, half)
    def _(q):
        sib_copy(q).start()

    for load in loads[1:]:
        load.wait()

    xcos, xsin = xtab.at[0], xtab.at[1]
    ycos, ysin = (lambda n: ytab[0, n]), (lambda n: ytab[1, n])
    diagonal = lax.broadcasted_iota(jnp.int32, (here, here), 0) == lax.broadcasted_iota(
        jnp.int32, (here, here), 1
    )

    def column(row):
        wide = jnp.broadcast_to(row[...].astype(F32), (here, here))
        return jnp.sum(jnp.where(diagonal, wide, 0.0), axis=1, keepdims=True)

    oid, sid, fixed = column(oid_row).astype(jnp.int32), column(sid_row).astype(jnp.int32), column(fixed_row)
    shift = jnp.broadcast_to(sid, (here, 128))
    at_x, at_y = shift & (TX - 1), shift >> 3
    twice = lambda v: jnp.concatenate([v, v], axis=1)
    wide_x = twice(at_x)

    def chosen(at, table, shape):
        out = jnp.zeros(shape, F32)
        for n in range(TX):
            out = jnp.where(at == n, table(n), out)
        return out

    def phase_y(line):
        c = chosen(at_y, lambda n: ycos(line * TY + n), (here, 128))
        s = chosen(at_y, lambda n: ysin(line * TY + n), (here, 128))
        return twice(c), twice(s)

    px_c = chosen(wide_x, lambda n: xcos[n : n + 1, :], (here, IMG))
    px_s = chosen(wide_x, lambda n: xsin[n : n + 1, :], (here, IMG))
    turn_c, turn_s = phase_y(1)

    def turned(line):
        c, s = phase_y(line)
        return px_c * c - px_s * s, px_s * c + px_c * s

    def band_of(i):
        low = wrap(i, half)
        hop = lax.div(low, 2)
        flip = low - 2 * hop
        to = jnp.where(i < half, me_l, 1 - me_l) * side + wrap(me_x + hop, side)
        return 2 * to + jnp.where(flip == 0, core, 1 - core)

    def row_copy(i):
        to = {"dom": band_of(i), "cls": jnp.where(i < NEAR_ROWS, me_c, other)}
        return send(out_rows.at[i], in_rows.at[:, me_d], row_s.at[i], row_r.at[i], to)

    @pl.loop(0, doms)
    def _(i):
        d = band_of(i)

        c, s = turned(d * lines)
        for r in range(lines):
            if r > 0:
                c, s = c * turn_c - s * turn_s, c * turn_s + s * turn_c
            col = pl.ds(pl.multiple_of(d * band + r * IMG, IMG), IMG)
            re, im = imgs[0, :, col].astype(F32), imgs[1, :, col].astype(F32)
            out_rows[i, 0, :, r * IMG : (r + 1) * IMG] = (re * c - im * s).astype(BF16)
            out_rows[i, 1, :, r * IMG : (r + 1) * IMG] = (re * s + im * c).astype(BF16)

        @pl.when(i > 0)
        def _():
            row_copy(i).start()

    in_rows[:, me_d] = out_rows[0]

    acc[...] = jnp.zeros_like(acc)
    xs_b[...] = jnp.zeros_like(xs_b)
    rs_b[...] = jnp.zeros_like(rs_b)

    def prepare(xs, rs, block, q):
        d = 2 * q + core
        col = pl.multiple_of(d * band + block * IMG, IMG)
        near = pl.ds(pl.multiple_of(block * IMG, IMG), IMG)
        for n in range(2):
            if n == 0:
                re, im = imgs[0, :, pl.ds(col, IMG)], imgs[1, :, pl.ds(col, IMG)]
            else:
                re, im = sib[q, 0, :, near], sib[q, 1, :, near]
            row = n * TX * here
            mid = row + TX // 2 * here
            xs[mid : mid + here, 0:IMG] = re
            xs[mid : mid + here, IMG:] = im
            re, im = re.astype(F32), im.astype(F32)
            for t in range(1, TX // 2 + 1):
                a = TX // 2 - t
                co, si = xcos[a : a + 1, :], xsin[a : a + 1, :]
                rc, rsn, ic, isn = re * co, re * si, im * co, im * si
                at = row + a * here
                xs[at : at + here, 0:IMG] = (rc - isn).astype(BF16)
                xs[at : at + here, IMG:] = (rsn + ic).astype(BF16)
                if t < TX // 2:
                    at = row + (TX // 2 + t) * here
                    xs[at : at + here, 0:IMG] = (rc + isn).astype(BF16)
                    xs[at : at + here, IMG:] = (ic - rsn).astype(BF16)
        re, im = ref_all[block, q, 0], ref_all[block, q, 1]
        mid = TY // 2 * columns
        rs[mid : mid + columns, 0:IMG] = re
        rs[mid : mid + columns, IMG:] = im
        re, im = re.astype(F32), im.astype(F32)
        ky = (d * lines + block) * TY
        for t in range(1, TY // 2 + 1):
            b = TY // 2 - t
            co, si = ycos(ky + b), ysin(ky + b)
            rc, rsn, ic, isn = re * co, re * si, im * co, im * si
            at = b * columns
            rs[at : at + columns, 0:IMG] = (rc + isn).astype(BF16)
            rs[at : at + columns, IMG:] = (ic - rsn).astype(BF16)
            if t < TY // 2:
                at = (TY // 2 + t) * columns
                rs[at : at + columns, 0:IMG] = (rc - isn).astype(BF16)
                rs[at : at + columns, IMG:] = (ic + rsn).astype(BF16)

    def add(xs, rs):
        acc[...] += lax.dot_general(
            xs[...], rs[...], (((1,), (1,)), ((), ())), preferred_element_type=F32
        )

    first, middle = half // 2, half * (steps - 1)

    @pl.loop(0, half + middle)
    def _(t):
        u = t - first
        s = 1
        for k in range(1, steps - 1):
            s = jnp.where(u >= k * half, k + 1, s)
        j = u - half * (s - 1)
        m = t - first - middle
        at_first, at_last = t < first, m >= 0
        j_a = jnp.where(at_last, m, jnp.where(at_first, 2 * t, j))
        j_b = jnp.where(at_last, m + half // 2, jnp.where(at_first, 2 * t + 1, j))

        @pl.when(at_first)
        def _():
            for c in (j_a, j_b):

                @pl.when(c > 0)
                def _():
                    plane_copy(c).wait_recv()
                    ring_copy(0, 1, c).start()
                    ring_copy(1, 1, c).start()

            for c in (j_a, j_b):
                sib_copy(piece(c)).wait()

        @pl.when((t >= first) & (m < 0))
        def _():
            ring_copy(0, s, j).wait_recv()

            @pl.when((s < steps - 1) | (j < half // 2))
            def _():
                ring_copy(0, s + 1, j).start()

            ring_copy(1, s, j).wait_recv()

            @pl.when((s < steps - 1) | (j >= half // 2))
            def _():
                ring_copy(1, s + 1, j).start()

        @pl.when(at_last)
        def _():
            ring_copy(0, steps, j_a).wait_recv()
            ring_copy(1, steps, j_b).wait_recv()

        near = jnp.where(at_last, steps, jnp.where(at_first, 0, s))
        prepare(xs_a, rs_a, wrap(me_z + zs - near, zs), piece(j_a))
        add(xs_b, rs_b)
        prepare(xs_b, rs_b, wrap(me_z + near, zs), piece(j_b))
        add(xs_a, rs_a)

    add(xs_b, rs_b)

    rows = TX * here
    swap = send(acc.at[pl.ds(rows, rows)], got, one_s.at[0], one_r.at[0], {"dom": twin})
    swap.start()
    swap.wait()
    logits = (acc[0:rows] + got[...]).reshape(TX, here, TY * columns)
    top = jnp.max(jnp.max(logits, axis=0), axis=1, keepdims=True)
    grown = jnp.sum(jnp.exp(logits - top[None]), axis=0)
    lane = lax.broadcasted_iota(jnp.int32, (here, TY * columns), 1)
    of_class = (lane // zs) % classes
    sums = [jnp.sum(jnp.where(of_class == k, grown, 0.0), axis=1, keepdims=True) for k in range(classes)]
    total = sums[0]
    for k in range(1, classes):
        total = total + sums[k]

    lane = lax.broadcasted_iota(jnp.int32, (here, 128), 1)
    fields = jnp.zeros((here, 128), F32)
    for n, v in enumerate((*sums, top, total, fixed, oid.astype(F32))):
        fields = jnp.where(lane == n, v, fields)
    fields = jnp.concatenate([fields, jnp.zeros((128 - here, 128), F32)], axis=0).T
    packs = 128 // here
    mark = lax.rem(me_d, packs) * here
    stat[...] = pltpu.roll(fields[0 : 2 * classes], mark, 1)

    def stat_copy(far, i):
        to = {"dom": wrap(me_d + i, doms), "cls": other} if far else {"dom": wrap(me_d + i, doms)}
        return send(stat, stat_in.at[me_c, me_d], mix_s.at[far, i], mix_r.at[far, i], to)

    @pl.loop(0, doms)
    def _(i):
        stat_copy(1, i).start()

        @pl.when(i > 0)
        def _():
            stat_copy(0, i).start()

    stat_in[me_c, me_d] = stat[...]

    @pl.loop(1, doms)
    def _(i):
        row_copy(i).wait()

    @pl.loop(0, doms)
    def _(i):
        stat_copy(1, i).wait()

        @pl.when(i > 0)
        def _():
            stat_copy(0, i).wait()

    def shares(mine, theirs):
        top_a, top_b = mine[classes : classes + 1], theirs[classes : classes + 1]
        both = jnp.maximum(top_a, top_b)
        scale = jnp.exp(top_a - both)
        total = mine[classes + 1 : classes + 2] * scale + theirs[classes + 1 : classes + 2] * jnp.exp(top_b - both)
        return mine[0:classes] * scale / total

    def joined(c):
        sums = [jnp.sum(stat_in[c, n : n + packs], axis=0) for n in range(0, doms, packs)]
        return jnp.concatenate(sums, axis=1)

    mine = joined(me_c)
    weight = (mine[classes + 2 : classes + 3] * shares(mine, joined(other))).astype(BF16).astype(F32)
    wide = 2 * classes
    of_entry = jnp.broadcast_to(mine[2 * classes - 1 :].astype(jnp.int32), (wide, doms * here))
    none = jnp.zeros_like(weight)

    def grow(part):
        rows = jnp.concatenate([weight, none] if part == 0 else [none, weight], axis=0)
        mixing = jnp.concatenate([jnp.where(of_entry == o, rows, 0.0) for o in range(zs)], axis=0)
        return jnp.dot(
            mixing.astype(BF16), in_rows[part].reshape(doms * here, band), preferred_element_type=F32
        )

    volume = grow(0) + grow(1)
    for o in range(zs):
        slab[o] = volume[o * wide : (o + 1) * wide].astype(BF16)

    def z_copy(i):
        return send(slab.at[wrap(me_z + i, zs)], slab_in.at[i], z_s.at[i], z_r.at[i], {"orient": wrap(me_z + i, zs)})

    for i in sorted(range(1, zs), key=lambda i: -min(i, zs - i)):
        z_copy(i).start()

    slab_in[0] = slab[me_z]
    live = lax.broadcasted_iota(jnp.int32, stat.shape, 1) - mark
    live = (live >= 0) & (live < here)
    prob = shares(jnp.where(live, stat[...], 1.0), jnp.where(live, stat_in[other, me_d], 1.0))
    prob = pltpu.roll(jnp.concatenate([prob, prob], axis=0), 128 - mark, 1)
    prob_out[...] = prob[0:classes, 0:here]

    @pl.loop(1, half)
    def _(j):
        plane_copy(j).wait_send()

    @pl.loop(0, steps * half)
    def _(n):
        s = 1 + lax.div(n, half)
        j = n - half * (s - 1)

        @pl.when((s < steps) | (j < half // 2))
        def _():
            ring_copy(0, s, j).wait_send()

        @pl.when((s < steps) | (j >= half // 2))
        def _():
            ring_copy(1, s, j).wait_send()

    @pl.loop(1, zs)
    def _(i):
        z_copy(i).wait()

    out = slab_in[0].astype(F32)
    for i in range(1, zs):
        out = out + slab_in[i].astype(F32)
    vol_out[...] = out


def tables():
    kx = np.arange(IMG) - IMG // 2
    ky = np.arange(IMG // 2)
    turn_x = 2 * np.pi / IMG * ((np.arange(TX) - TX // 2)[:, None] * kx[None, :])
    turn_y = 2 * np.pi / IMG * (ky[:, None] * (np.arange(TY) - TY // 2)[None, :])
    return [
        np.stack([np.cos(t), np.sin(t)]).astype(np.float32) for t in (turn_x, turn_y.reshape(-1))
    ]


def solution(mesh):
    doms, zs = mesh.shape["dom"], mesh.shape["orient"]

    def local(references, images, orient_lists, shift_ids, fixed_weights):
        classes, here = references.shape[1], images.shape[1]
        columns = classes * references.shape[2]
        band = images.shape[2] // doms
        half = doms // 2
        vmem, hbm = pl.BlockSpec(memory_space=pltpu.VMEM), pl.BlockSpec(memory_space=pltpu.MemorySpace.HBM)
        dma = pltpu.SemaphoreType.DMA
        rows = TX * here
        prob, volume = pl.pallas_call(
            functools.partial(kernel, doms, zs),
            out_shape=(
                jax.ShapeDtypeStruct((classes, here), F32),
                jax.ShapeDtypeStruct((2 * classes, band), F32),
            ),
            in_specs=[hbm] * 7,
            out_specs=(vmem, vmem),
            scratch_shapes=[
                pltpu.VMEM((2, here, images.shape[2]), BF16),
                pltpu.VMEM((2, TX, IMG), F32),
                pltpu.SMEM((2, IMG // 2 * TY), F32),
                pltpu.VMEM((1, here), jnp.int32),
                pltpu.VMEM((1, here), jnp.int32),
                pltpu.VMEM((1, here), F32),
                pltpu.VMEM((zs, half, 2, columns, IMG), BF16),
                pltpu.VMEM((half, 2, here, band), BF16),
                pltpu.VMEM((doms, 2, here, band), BF16),
                pltpu.VMEM((2, doms, here, band), BF16),
                pltpu.VMEM((2 * rows, 2 * IMG), BF16),
                pltpu.VMEM((TY * columns, 2 * IMG), BF16),
                pltpu.VMEM((2 * rows, 2 * IMG), BF16),
                pltpu.VMEM((TY * columns, 2 * IMG), BF16),
                pltpu.VMEM((2 * rows, TY * columns), F32),
                pltpu.VMEM((rows, TY * columns), F32),
                pltpu.VMEM((2 * classes, 128), F32),
                pltpu.VMEM((2, doms, 2 * classes, 128), F32),
                pltpu.VMEM((zs, 2 * classes, band), BF16),
                pltpu.VMEM((zs, 2 * classes, band), BF16),
                dma((half,)), dma((half,)),
                dma((half,)), dma((half,)),
                dma((doms,)), dma((doms,)),
                dma((2, zs // 2, half)), dma((2, zs // 2, half)),
                dma((1,)), dma((1,)),
                dma((2, doms)), dma((2, doms)),
                dma((zs,)), dma((zs,)),
                dma((7,)),
            ],
            compiler_params=pltpu.CompilerParams(
                collective_id=0, has_side_effects=True, vmem_limit_bytes=48 << 20
            ),
            name="estep",
        )(
            *[
                pltpu.with_memory_space_constraint(v, pltpu.MemorySpace.HBM)
                for v in (
                    references.reshape(2, columns, references.shape[3]),
                    images,
                    *[jnp.asarray(t) for t in tables()],
                    orient_lists.reshape(1, here),
                    shift_ids.reshape(1, here),
                    fixed_weights.reshape(1, here),
                )
            ]
        )
        return prob.T, volume.reshape(2, classes, 1, band)

    in_specs = (
        P(None, "cls", None, ("dom", "orient")),
        P(None, ("dom", "orient"), None),
        P(("dom", "orient"), None),
        P(("dom", "orient"), None),
        P(("dom", "orient"), None),
    )
    out_specs = (P(("dom", "orient"), "cls"), P(None, "cls", "orient", "dom"))
    return jax.shard_map(local, mesh=mesh, in_specs=in_specs, out_specs=out_specs, check_vma=False)
```

```python
import functools
import math

import jax
import jax.numpy as jnp
import numpy as np
from jax import lax
from jax.experimental import pallas as pl
from jax.experimental.pallas import tpu as pltpu
from jax.sharding import PartitionSpec as P

IMG = 256
TX = 8
TY = 8
MESH = pl.DeviceIdType.MESH
F32 = jnp.float32
BF16 = jnp.bfloat16


def kernel(
    doms, zs, refs, images, xtab_in, ytab_in, oid_in, sid_in, fixed_in, prob_out, vol_out,
    imgs, xtab, ytab, oid_row, sid_row, fixed_row,
    ref_all, sib, out_rows, in_rows, xs_a, rs_a, xs_b, rs_b, acc, got, stat, stat_in, slab, slab_in,
    plane_s, plane_r, sib_s, sib_r, row_s, row_r, ring_s, ring_r, one_s, one_r, mix_s, mix_r, z_s, z_r, in_s,
):
    here = images.shape[1]
    band = images.shape[2] // doms
    lines = band // IMG
    half = doms // 2
    side = half // 2
    columns = refs.shape[1]
    classes = columns // zs
    steps = zs // 2
    me_d, me_z, me_c = lax.axis_index("dom"), lax.axis_index("orient"), lax.axis_index("cls")
    core, me_q = lax.rem(me_d, 2), lax.div(me_d, 2)
    me_x, me_l = lax.rem(me_q, side), lax.div(me_q, side)
    twin = me_d + 1 - 2 * core

    def wrap(v, n):
        return jnp.where(v >= n, v - n, v)

    other = 1 - me_c

    def send(src, dst, s, r, to):
        return pltpu.make_async_remote_copy(
            src_ref=src, dst_ref=dst, send_sem=s, recv_sem=r, device_id=to, device_id_type=MESH
        )

    barrier = pltpu.get_barrier_semaphore()

    def greet(to):
        pl.semaphore_signal(barrier, inc=1, device_id=to, device_id_type=MESH)

    @pl.loop(1, doms)
    def _(i):
        greet({"dom": wrap(me_d + i, doms)})

    @pl.loop(1, zs)
    def _(i):
        greet({"orient": wrap(me_z + i, zs)})

    @pl.loop(0, doms)
    def _(i):
        greet({"dom": i, "cls": other})

    loads = [
        pltpu.make_async_copy(src, dst, in_s.at[n])
        for n, (src, dst) in enumerate(
            (
                (refs, ref_all.at[me_z, me_q]),
                (images, imgs),
                (xtab_in, xtab),
                (ytab_in, ytab),
                (oid_in, oid_row),
                (sid_in, sid_row),
                (fixed_in, fixed_row),
            )
        )
    ]
    for load in loads:
        load.start()
    pl.semaphore_wait(barrier, 2 * doms + zs - 2)

    def plane_copy(j):
        low = wrap(j, side)
        to = jnp.where(j < side, me_l, 1 - me_l) * side + wrap(me_x + low, side)
        at = ref_all.at[me_z, me_q]
        return send(at, at, plane_s.at[j], plane_r.at[j], {"dom": 2 * to + core})

    def piece(j):
        low = wrap(j, side)
        return jnp.where(j < side, me_l, 1 - me_l) * side + wrap(me_x + side - low, side)

    def sib_copy(q):
        start = pl.multiple_of((2 * q + 1 - core) * band, band)
        return send(images.at[:, :, pl.ds(start, band)], sib.at[q], sib_s.at[q], sib_r.at[q], {"dom": twin})

    right, left = wrap(me_z + 1, zs), wrap(me_z + zs - 1, zs)

    def ring_copy(way, s, j):
        block = wrap(me_z + zs + 1 - s, zs) if way == 0 else wrap(me_z + s - 1, zs)
        at = ref_all.at[block, piece(j)]
        return send(
            at, at, ring_s.at[way, s - 1, j], ring_r.at[way, s - 1, j], {"orient": right if way == 0 else left}
        )

    loads[0].wait()
    ring_copy(0, 1, 0).start()
    ring_copy(1, 1, 0).start()

    @pl.loop(1, half)
    def _(j):
        plane_copy(j).start()

    @pl.loop(0, half)
    def _(q):
        sib_copy(q).start()

    for load in loads[1:]:
        load.wait()

    xcos, xsin = xtab.at[0], xtab.at[1]
    ycos, ysin = (lambda n: ytab[0, n]), (lambda n: ytab[1, n])
    diagonal = lax.broadcasted_iota(jnp.int32, (here, here), 0) == lax.broadcasted_iota(
        jnp.int32, (here, here), 1
    )

    def column(row):
        wide = jnp.broadcast_to(row[...].astype(F32), (here, here))
        return jnp.sum(jnp.where(diagonal, wide, 0.0), axis=1, keepdims=True)

    oid, sid, fixed = column(oid_row).astype(jnp.int32), column(sid_row).astype(jnp.int32), column(fixed_row)
    shift = jnp.broadcast_to(sid, (here, 128))
    at_x, at_y = shift & (TX - 1), shift >> 3
    twice = lambda v: jnp.concatenate([v, v], axis=1)
    wide_x = twice(at_x)

    def chosen(at, table, shape):
        out = jnp.zeros(shape, F32)
        for n in range(TX):
            out = jnp.where(at == n, table(n), out)
        return out

    def phase_y(line):
        c = chosen(at_y, lambda n: ycos(line * TY + n), (here, 128))
        s = chosen(at_y, lambda n: ysin(line * TY + n), (here, 128))
        return twice(c), twice(s)

    px_c = chosen(wide_x, lambda n: xcos[n : n + 1, :], (here, IMG))
    px_s = chosen(wide_x, lambda n: xsin[n : n + 1, :], (here, IMG))
    turn_c, turn_s = phase_y(1)

    def turned(line):
        c, s = phase_y(line)
        return px_c * c - px_s * s, px_s * c + px_c * s

    def band_of(i):
        low = wrap(i, half)
        hop = lax.div(low, 2)
        flip = low - 2 * hop
        to = jnp.where(i < half, me_l, 1 - me_l) * side + wrap(me_x + hop, side)
        return 2 * to + jnp.where(flip == 0, core, 1 - core)

    def row_copy(i):
        return send(out_rows.at[i], in_rows.at[:, me_d], row_s.at[i], row_r.at[i], {"dom": band_of(i)})

    me_y = 2 * me_c + me_l
    cls_of = [lax.div(wrap(me_y + 1, 4), 2), lax.div(wrap(me_y + 3, 4), 2)]

    def part_copy(i, r):
        n = i + r * half
        return send(
            out_rows.at[i, r], in_rows.at[r, me_d], row_s.at[n], row_r.at[n], {"dom": band_of(i), "cls": cls_of[r]}
        )

    @pl.loop(0, doms)
    def _(i):
        d = band_of(i)

        c, s = turned(d * lines)
        for r in range(lines):
            if r > 0:
                c, s = c * turn_c - s * turn_s, c * turn_s + s * turn_c
            col = pl.ds(pl.multiple_of(d * band + r * IMG, IMG), IMG)
            re, im = imgs[0, :, col].astype(F32), imgs[1, :, col].astype(F32)
            out_rows[i, 0, :, r * IMG : (r + 1) * IMG] = (re * c - im * s).astype(BF16)
            out_rows[i, 1, :, r * IMG : (r + 1) * IMG] = (re * s + im * c).astype(BF16)

        @pl.when((i > 0) & (i < half))
        def _():
            row_copy(i).start()

        @pl.when(i >= half)
        def _():
            part_copy(i, 0).start()
            part_copy(i, 1).start()

    in_rows[:, me_d] = out_rows[0]

    acc[...] = jnp.zeros_like(acc)
    xs_b[...] = jnp.zeros_like(xs_b)
    rs_b[...] = jnp.zeros_like(rs_b)

    def prepare(xs, rs, block, q):
        d = 2 * q + core
        col = pl.multiple_of(d * band + block * IMG, IMG)
        near = pl.ds(pl.multiple_of(block * IMG, IMG), IMG)
        for n in range(2):
            if n == 0:
                re, im = imgs[0, :, pl.ds(col, IMG)], imgs[1, :, pl.ds(col, IMG)]
            else:
                re, im = sib[q, 0, :, near], sib[q, 1, :, near]
            row = n * TX * here
            mid = row + TX // 2 * here
            xs[mid : mid + here, 0:IMG] = re
            xs[mid : mid + here, IMG:] = im
            re, im = re.astype(F32), im.astype(F32)
            for t in range(1, TX // 2 + 1):
                a = TX // 2 - t
                co, si = xcos[a : a + 1, :], xsin[a : a + 1, :]
                rc, rsn, ic, isn = re * co, re * si, im * co, im * si
                at = row + a * here
                xs[at : at + here, 0:IMG] = (rc - isn).astype(BF16)
                xs[at : at + here, IMG:] = (rsn + ic).astype(BF16)
                if t < TX // 2:
                    at = row + (TX // 2 + t) * here
                    xs[at : at + here, 0:IMG] = (rc + isn).astype(BF16)
                    xs[at : at + here, IMG:] = (ic - rsn).astype(BF16)
        re, im = ref_all[block, q, 0], ref_all[block, q, 1]
        mid = TY // 2 * columns
        rs[mid : mid + columns, 0:IMG] = re
        rs[mid : mid + columns, IMG:] = im
        re, im = re.astype(F32), im.astype(F32)
        ky = (d * lines + block) * TY
        for t in range(1, TY // 2 + 1):
            b = TY // 2 - t
            co, si = ycos(ky + b), ysin(ky + b)
            rc, rsn, ic, isn = re * co, re * si, im * co, im * si
            at = b * columns
            rs[at : at + columns, 0:IMG] = (rc + isn).astype(BF16)
            rs[at : at + columns, IMG:] = (ic - rsn).astype(BF16)
            if t < TY // 2:
                at = (TY // 2 + t) * columns
                rs[at : at + columns, 0:IMG] = (rc - isn).astype(BF16)
                rs[at : at + columns, IMG:] = (ic + rsn).astype(BF16)

    def add(xs, rs):
        acc[...] += lax.dot_general(
            xs[...], rs[...], (((1,), (1,)), ((), ())), preferred_element_type=F32
        )

    first, middle = half // 2, half * (steps - 1)

    @pl.loop(0, half + middle)
    def _(t):
        u = t - first
        s = 1
        for k in range(1, steps - 1):
            s = jnp.where(u >= k * half, k + 1, s)
        j = u - half * (s - 1)
        m = t - first - middle
        at_first, at_last = t < first, m >= 0
        j_a = jnp.where(at_last, m, jnp.where(at_first, 2 * t, j))
        j_b = jnp.where(at_last, m + half // 2, jnp.where(at_first, 2 * t + 1, j))

        @pl.when(at_first)
        def _():
            for c in (j_a, j_b):

                @pl.when(c > 0)
                def _():
                    plane_copy(c).wait_recv()
                    ring_copy(0, 1, c).start()
                    ring_copy(1, 1, c).start()

            for c in (j_a, j_b):
                sib_copy(piece(c)).wait()

        @pl.when((t >= first) & (m < 0))
        def _():
            ring_copy(0, s, j).wait_recv()

            @pl.when((s < steps - 1) | (j < half // 2))
            def _():
                ring_copy(0, s + 1, j).start()

            ring_copy(1, s, j).wait_recv()

            @pl.when((s < steps - 1) | (j >= half // 2))
            def _():
                ring_copy(1, s + 1, j).start()

        @pl.when(at_last)
        def _():
            ring_copy(0, steps, j_a).wait_recv()
            ring_copy(1, steps, j_b).wait_recv()

        near = jnp.where(at_last, steps, jnp.where(at_first, 0, s))
        prepare(xs_a, rs_a, wrap(me_z + zs - near, zs), piece(j_a))
        add(xs_b, rs_b)
        prepare(xs_b, rs_b, wrap(me_z + near, zs), piece(j_b))
        add(xs_a, rs_a)

    add(xs_b, rs_b)

    rows = TX * here
    swap = send(acc.at[pl.ds(rows, rows)], got, one_s.at[0], one_r.at[0], {"dom": twin})
    swap.start()
    swap.wait()
    logits = (acc[0:rows] + got[...]).reshape(TX, here, TY * columns)
    top = jnp.max(jnp.max(logits, axis=0), axis=1, keepdims=True)
    grown = jnp.sum(jnp.exp(logits - top[None]), axis=0)
    lane = lax.broadcasted_iota(jnp.int32, (here, TY * columns), 1)
    of_class = (lane // zs) % classes
    sums = [jnp.sum(jnp.where(of_class == k, grown, 0.0), axis=1, keepdims=True) for k in range(classes)]
    total = sums[0]
    for k in range(1, classes):
        total = total + sums[k]

    lane = lax.broadcasted_iota(jnp.int32, (here, 128), 1)
    fields = jnp.zeros((here, 128), F32)
    for n, v in enumerate((*sums, top, total, fixed, oid.astype(F32))):
        fields = jnp.where(lane == n, v, fields)
    fields = jnp.concatenate([fields, jnp.zeros((128 - here, 128), F32)], axis=0).T
    kinds = 2 * classes
    stat[...] = jnp.sum(pltpu.roll(fields[0:kinds], 0, 1, stride=here, stride_axis=0), axis=0, keepdims=True)

    def stat_copy(far, i):
        to = {"dom": wrap(me_d + i, doms), "cls": other} if far else {"dom": wrap(me_d + i, doms)}
        return send(stat, stat_in.at[me_c, me_d], mix_s.at[far, i], mix_r.at[far, i], to)

    @pl.loop(0, doms)
    def _(i):
        stat_copy(1, i).start()

        @pl.when(i > 0)
        def _():
            stat_copy(0, i).start()

    stat_in[me_c, me_d] = stat[...]

    @pl.loop(1, half)
    def _(i):
        row_copy(i).wait()

    @pl.loop(half, doms)
    def _(i):
        part_copy(i, 0).wait()
        part_copy(i, 1).wait()

    @pl.loop(0, doms)
    def _(i):
        stat_copy(1, i).wait()

        @pl.when(i > 0)
        def _():
            stat_copy(0, i).wait()

    packs = 128 // here
    of_sender = lax.broadcasted_iota(jnp.int32, (packs, 128), 1) // here == lax.broadcasted_iota(
        jnp.int32, (packs, 128), 0
    )

    def unpacked(c, names):
        tiles = [stat_in[c, n : n + packs].reshape(packs, 128) for n in range(0, doms, packs)]

        def field(f):
            turned = [pltpu.roll(v, (128 - f * here) % 128, 1) for v in tiles]
            turned = [pltpu.roll(v, 0, 1, stride=here, stride_axis=0) for v in turned]
            return jnp.concatenate(
                [jnp.sum(jnp.where(of_sender, v, 0.0), axis=0, keepdims=True) for v in turned], axis=1
            )

        return [field(f) for f in names]

    def norm(top_a, total_a, top_b, total_b):
        both = jnp.maximum(top_a, top_b)
        scale = jnp.exp(top_a - both)
        return scale, total_a * scale + total_b * jnp.exp(top_b - both)

    *mine, top_a, total_a, fixed_a, oid_a = unpacked(me_c, range(kinds))
    scale, total = norm(top_a, total_a, *unpacked(other, (classes, classes + 1)))
    mine = jnp.concatenate(mine, axis=0)
    weight = (fixed_a * (mine * scale / total)).astype(BF16).astype(F32)
    wide = 2 * classes
    of_entry = jnp.broadcast_to(oid_a.astype(jnp.int32), (wide, doms * here))
    none = jnp.zeros_like(weight)

    def grow(part):
        rows = jnp.concatenate([weight, none] if part == 0 else [none, weight], axis=0)
        mixing = jnp.concatenate([jnp.where(of_entry == o, rows, 0.0) for o in range(zs)], axis=0)
        return jnp.dot(
            mixing.astype(BF16), in_rows[part].reshape(doms * here, band), preferred_element_type=F32
        )

    volume = grow(0) + grow(1)
    for o in range(zs):
        slab[o] = volume[o * wide : (o + 1) * wide].astype(BF16)

    def z_copy(i):
        return send(slab.at[wrap(me_z + i, zs)], slab_in.at[i], z_s.at[i], z_r.at[i], {"orient": wrap(me_z + i, zs)})

    for i in sorted(range(1, zs), key=lambda i: -min(i, zs - i)):
        z_copy(i).start()

    slab_in[0] = slab[me_z]
    own, far = stat[...], stat_in[other, me_d]
    cut = lambda row, f: row[:, f * here : (f + 1) * here]
    scale, total = norm(cut(own, classes), cut(own, classes + 1), cut(far, classes), cut(far, classes + 1))
    for k in range(classes):
        prob_out[k : k + 1, :] = cut(own, k) * scale / total

    @pl.loop(1, half)
    def _(j):
        plane_copy(j).wait_send()

    @pl.loop(0, steps * half)
    def _(n):
        s = 1 + lax.div(n, half)
        j = n - half * (s - 1)

        @pl.when((s < steps) | (j < half // 2))
        def _():
            ring_copy(0, s, j).wait_send()

        @pl.when((s < steps) | (j >= half // 2))
        def _():
            ring_copy(1, s, j).wait_send()

    @pl.loop(1, zs)
    def _(i):
        z_copy(i).wait()

    out = slab_in[0].astype(F32)
    for i in range(1, zs):
        out = out + slab_in[i].astype(F32)
    vol_out[...] = out


def tables():
    kx = np.arange(IMG) - IMG // 2
    ky = np.arange(IMG // 2)
    turn_x = 2 * np.pi / IMG * ((np.arange(TX) - TX // 2)[:, None] * kx[None, :])
    turn_y = 2 * np.pi / IMG * (ky[:, None] * (np.arange(TY) - TY // 2)[None, :])
    return [
        np.stack([np.cos(t), np.sin(t)]).astype(np.float32) for t in (turn_x, turn_y.reshape(-1))
    ]


def solution(mesh):
    doms, zs = mesh.shape["dom"], mesh.shape["orient"]

    def local(references, images, orient_lists, shift_ids, fixed_weights):
        classes, here = references.shape[1], images.shape[1]
        columns = classes * references.shape[2]
        band = images.shape[2] // doms
        half = doms // 2
        vmem, hbm = pl.BlockSpec(memory_space=pltpu.VMEM), pl.BlockSpec(memory_space=pltpu.MemorySpace.HBM)
        dma = pltpu.SemaphoreType.DMA
        rows = TX * here
        prob, volume = pl.pallas_call(
            functools.partial(kernel, doms, zs),
            out_shape=(
                jax.ShapeDtypeStruct((classes, here), F32),
                jax.ShapeDtypeStruct((2 * classes, band), F32),
            ),
            in_specs=[hbm] * 7,
            out_specs=(vmem, vmem),
            scratch_shapes=[
                pltpu.VMEM((2, here, images.shape[2]), BF16),
                pltpu.VMEM((2, TX, IMG), F32),
                pltpu.SMEM((2, IMG // 2 * TY), F32),
                pltpu.VMEM((1, here), jnp.int32),
                pltpu.VMEM((1, here), jnp.int32),
                pltpu.VMEM((1, here), F32),
                pltpu.VMEM((zs, half, 2, columns, IMG), BF16),
                pltpu.VMEM((half, 2, here, band), BF16),
                pltpu.VMEM((doms, 2, here, band), BF16),
                pltpu.VMEM((2, doms, here, band), BF16),
                pltpu.VMEM((2 * rows, 2 * IMG), BF16),
                pltpu.VMEM((TY * columns, 2 * IMG), BF16),
                pltpu.VMEM((2 * rows, 2 * IMG), BF16),
                pltpu.VMEM((TY * columns, 2 * IMG), BF16),
                pltpu.VMEM((2 * rows, TY * columns), F32),
                pltpu.VMEM((rows, TY * columns), F32),
                pltpu.VMEM((1, 128), F32),
                pltpu.VMEM((2, doms, 1, 128), F32),
                pltpu.VMEM((zs, 2 * classes, band), BF16),
                pltpu.VMEM((zs, 2 * classes, band), BF16),
                dma((half,)), dma((half,)),
                dma((half,)), dma((half,)),
                dma((doms + half,)), dma((doms + half,)),
                dma((2, zs // 2, half)), dma((2, zs // 2, half)),
                dma((1,)), dma((1,)),
                dma((2, doms)), dma((2, doms)),
                dma((zs,)), dma((zs,)),
                dma((7,)),
            ],
            compiler_params=pltpu.CompilerParams(
                collective_id=0, has_side_effects=True, vmem_limit_bytes=48 << 20
            ),
            name="estep",
        )(
            *[
                pltpu.with_memory_space_constraint(v, pltpu.MemorySpace.HBM)
                for v in (
                    references.reshape(2, columns, references.shape[3]),
                    images,
                    *[jnp.asarray(t) for t in tables()],
                    orient_lists.reshape(1, here),
                    shift_ids.reshape(1, here),
                    fixed_weights.reshape(1, here),
                )
            ]
        )
        return prob.T, volume.reshape(2, classes, 1, band)

    in_specs = (
        P(None, "cls", None, ("dom", "orient")),
        P(None, ("dom", "orient"), None),
        P(("dom", "orient"), None),
        P(("dom", "orient"), None),
        P(("dom", "orient"), None),
    )
    out_specs = (P(("dom", "orient"), "cls"), P(None, "cls", "orient", "dom"))
    return jax.shard_map(local, mesh=mesh, in_specs=in_specs, out_specs=out_specs, check_vma=False)
```

```python
import functools
import math

import jax
import jax.numpy as jnp
import numpy as np
from jax import lax
from jax.experimental import pallas as pl
from jax.experimental.pallas import tpu as pltpu
from jax.sharding import PartitionSpec as P

IMG = 256
TX = 8
TY = 8
MESH = pl.DeviceIdType.MESH
F32 = jnp.float32
BF16 = jnp.bfloat16


def kernel(
    doms, zs, refs, images, xtab_in, ytab_in, oid_in, sid_in, fixed_in, prob_out, vol_out,
    imgs, xtab, ytab, oid_row, sid_row, fixed_row,
    ref_all, sib, out_rows, in_rows, xs_a, rs_a, xs_b, rs_b, acc, got, stat, stat_in, slab, slab_in,
    plane_s, plane_r, sib_s, sib_r, row_s, row_r, ring_s, ring_r, one_s, one_r, mix_s, mix_r, z_s, z_r, in_s,
):
    here = images.shape[1]
    band = images.shape[2] // doms
    lines = band // IMG
    half = doms // 2
    side = half // 2
    columns = refs.shape[1]
    classes = columns // zs
    steps = zs // 2
    me_d, me_z, me_c = lax.axis_index("dom"), lax.axis_index("orient"), lax.axis_index("cls")
    core, me_q = lax.rem(me_d, 2), lax.div(me_d, 2)
    me_x, me_l = lax.rem(me_q, side), lax.div(me_q, side)
    twin = me_d + 1 - 2 * core

    def wrap(v, n):
        return jnp.where(v >= n, v - n, v)

    other = 1 - me_c

    def send(src, dst, s, r, to):
        return pltpu.make_async_remote_copy(
            src_ref=src, dst_ref=dst, send_sem=s, recv_sem=r, device_id=to, device_id_type=MESH
        )

    barrier = pltpu.get_barrier_semaphore()

    def greet(to):
        pl.semaphore_signal(barrier, inc=1, device_id=to, device_id_type=MESH)

    @pl.loop(1, doms)
    def _(i):
        greet({"dom": wrap(me_d + i, doms)})

    @pl.loop(1, zs)
    def _(i):
        greet({"orient": wrap(me_z + i, zs)})

    @pl.loop(0, doms)
    def _(i):
        greet({"dom": i, "cls": other})

    loads = [
        pltpu.make_async_copy(src, dst, in_s.at[n])
        for n, (src, dst) in enumerate(
            (
                (refs, ref_all.at[me_z, me_q]),
                (images, imgs),
                (xtab_in, xtab),
                (ytab_in, ytab),
                (oid_in, oid_row),
                (sid_in, sid_row),
                (fixed_in, fixed_row),
            )
        )
    ]
    for load in loads:
        load.start()
    pl.semaphore_wait(barrier, 2 * doms + zs - 2)

    def plane_copy(j):
        low = wrap(j, side)
        to = jnp.where(j < side, me_l, 1 - me_l) * side + wrap(me_x + low, side)
        at = ref_all.at[me_z, me_q]
        return send(at, at, plane_s.at[j], plane_r.at[j], {"dom": 2 * to + core})

    def piece(j):
        low = wrap(j, side)
        return jnp.where(j < side, me_l, 1 - me_l) * side + wrap(me_x + side - low, side)

    def sib_copy(q):
        start = pl.multiple_of((2 * q + 1 - core) * band, band)
        return send(images.at[:, :, pl.ds(start, band)], sib.at[q], sib_s.at[q], sib_r.at[q], {"dom": twin})

    right, left = wrap(me_z + 1, zs), wrap(me_z + zs - 1, zs)

    def ring_copy(way, s, j):
        block = wrap(me_z + zs + 1 - s, zs) if way == 0 else wrap(me_z + s - 1, zs)
        at = ref_all.at[block, piece(j)]
        return send(
            at, at, ring_s.at[way, s - 1, j], ring_r.at[way, s - 1, j], {"orient": right if way == 0 else left}
        )

    loads[0].wait()
    ring_copy(0, 1, 0).start()
    ring_copy(1, 1, 0).start()

    @pl.loop(1, half)
    def _(j):
        plane_copy(j).start()

    @pl.loop(0, half)
    def _(j):
        sib_copy(piece(j)).start()

    for load in loads[1:]:
        load.wait()

    xcos, xsin = xtab.at[0], xtab.at[1]
    ycos, ysin = (lambda n: ytab[0, n]), (lambda n: ytab[1, n])
    diagonal = lax.broadcasted_iota(jnp.int32, (here, here), 0) == lax.broadcasted_iota(
        jnp.int32, (here, here), 1
    )

    def column(row):
        wide = jnp.broadcast_to(row[...].astype(F32), (here, here))
        return jnp.sum(jnp.where(diagonal, wide, 0.0), axis=1, keepdims=True)

    oid, sid, fixed = column(oid_row).astype(jnp.int32), column(sid_row).astype(jnp.int32), column(fixed_row)
    shift = jnp.broadcast_to(sid, (here, 128))
    at_x, at_y = shift & (TX - 1), shift >> 3
    twice = lambda v: jnp.concatenate([v, v], axis=1)
    wide_x = twice(at_x)

    def chosen(at, table, shape):
        out = jnp.zeros(shape, F32)
        for n in range(TX):
            out = jnp.where(at == n, table(n), out)
        return out

    def phase_y(line):
        c = chosen(at_y, lambda n: ycos(line * TY + n), (here, 128))
        s = chosen(at_y, lambda n: ysin(line * TY + n), (here, 128))
        return twice(c), twice(s)

    px_c = chosen(wide_x, lambda n: xcos[n : n + 1, :], (here, IMG))
    px_s = chosen(wide_x, lambda n: xsin[n : n + 1, :], (here, IMG))
    turn_c, turn_s = phase_y(1)

    def turned(line):
        c, s = phase_y(line)
        return px_c * c - px_s * s, px_s * c + px_c * s

    def band_of(i):
        low = wrap(i, half)
        hop = lax.div(low, 2)
        flip = low - 2 * hop
        to = jnp.where(i < half, me_l, 1 - me_l) * side + wrap(me_x + hop, side)
        return 2 * to + jnp.where(flip == 0, core, 1 - core)

    def row_copy(i):
        return send(out_rows.at[i], in_rows.at[:, me_d], row_s.at[i], row_r.at[i], {"dom": band_of(i)})

    me_y = 2 * me_c + me_l
    cls_of = [lax.div(wrap(me_y + 1, 4), 2), lax.div(wrap(me_y + 3, 4), 2)]

    def part_copy(i, r):
        n = i + r * half
        return send(
            out_rows.at[i, r], in_rows.at[r, me_d], row_s.at[n], row_r.at[n], {"dom": band_of(i), "cls": cls_of[r]}
        )

    @pl.loop(0, doms)
    def _(i):
        d = band_of(i)

        c, s = turned(d * lines)
        for r in range(lines):
            if r > 0:
                c, s = c * turn_c - s * turn_s, c * turn_s + s * turn_c
            col = pl.ds(pl.multiple_of(d * band + r * IMG, IMG), IMG)
            re, im = imgs[0, :, col].astype(F32), imgs[1, :, col].astype(F32)
            out_rows[i, 0, :, r * IMG : (r + 1) * IMG] = (re * c - im * s).astype(BF16)
            out_rows[i, 1, :, r * IMG : (r + 1) * IMG] = (re * s + im * c).astype(BF16)

        @pl.when((i > 0) & (i < half))
        def _():
            row_copy(i).start()

        @pl.when(i >= half)
        def _():
            part_copy(i, 0).start()
            part_copy(i, 1).start()

    in_rows[:, me_d] = out_rows[0]

    acc[...] = jnp.zeros_like(acc)
    xs_b[...] = jnp.zeros_like(xs_b)
    rs_b[...] = jnp.zeros_like(rs_b)

    def prepare(xs, rs, block, q):
        d = 2 * q + core
        col = pl.multiple_of(d * band + block * IMG, IMG)
        near = pl.ds(pl.multiple_of(block * IMG, IMG), IMG)
        for n in range(2):
            if n == 0:
                re, im = imgs[0, :, pl.ds(col, IMG)], imgs[1, :, pl.ds(col, IMG)]
            else:
                re, im = sib[q, 0, :, near], sib[q, 1, :, near]
            row = n * TX * here
            mid = row + TX // 2 * here
            xs[mid : mid + here, 0:IMG] = re
            xs[mid : mid + here, IMG:] = im
            re, im = re.astype(F32), im.astype(F32)
            for t in range(1, TX // 2 + 1):
                a = TX // 2 - t
                co, si = xcos[a : a + 1, :], xsin[a : a + 1, :]
                rc, rsn, ic, isn = re * co, re * si, im * co, im * si
                at = row + a * here
                xs[at : at + here, 0:IMG] = (rc - isn).astype(BF16)
                xs[at : at + here, IMG:] = (rsn + ic).astype(BF16)
                if t < TX // 2:
                    at = row + (TX // 2 + t) * here
                    xs[at : at + here, 0:IMG] = (rc + isn).astype(BF16)
                    xs[at : at + here, IMG:] = (ic - rsn).astype(BF16)
        re, im = ref_all[block, q, 0], ref_all[block, q, 1]
        mid = TY // 2 * columns
        rs[mid : mid + columns, 0:IMG] = re
        rs[mid : mid + columns, IMG:] = im
        re, im = re.astype(F32), im.astype(F32)
        ky = (d * lines + block) * TY
        for t in range(1, TY // 2 + 1):
            b = TY // 2 - t
            co, si = ycos(ky + b), ysin(ky + b)
            rc, rsn, ic, isn = re * co, re * si, im * co, im * si
            at = b * columns
            rs[at : at + columns, 0:IMG] = (rc + isn).astype(BF16)
            rs[at : at + columns, IMG:] = (ic - rsn).astype(BF16)
            if t < TY // 2:
                at = (TY // 2 + t) * columns
                rs[at : at + columns, 0:IMG] = (rc - isn).astype(BF16)
                rs[at : at + columns, IMG:] = (ic + rsn).astype(BF16)

    def add(xs, rs):
        acc[...] += lax.dot_general(
            xs[...], rs[...], (((1,), (1,)), ((), ())), preferred_element_type=F32
        )

    first, middle = half // 2, half * (steps - 1)

    @pl.loop(0, half + middle)
    def _(t):
        u = t - first
        s = 1
        for k in range(1, steps - 1):
            s = jnp.where(u >= k * half, k + 1, s)
        j = u - half * (s - 1)
        m = t - first - middle
        at_first, at_last = t < first, m >= 0
        j_a = jnp.where(at_last, m, jnp.where(at_first, 2 * t, j))
        j_b = jnp.where(at_last, m + half // 2, jnp.where(at_first, 2 * t + 1, j))

        @pl.when(at_first)
        def _():
            for c in (j_a, j_b):

                @pl.when(c > 0)
                def _():
                    plane_copy(c).wait_recv()
                    ring_copy(0, 1, c).start()
                    ring_copy(1, 1, c).start()

            for c in (j_a, j_b):
                sib_copy(piece(c)).wait()

        @pl.when((t >= first) & (m < 0))
        def _():
            ring_copy(0, s, j).wait_recv()

            @pl.when((s < steps - 1) | (j < half // 2))
            def _():
                ring_copy(0, s + 1, j).start()

            ring_copy(1, s, j).wait_recv()

            @pl.when((s < steps - 1) | (j >= half // 2))
            def _():
                ring_copy(1, s + 1, j).start()

        @pl.when(at_last)
        def _():
            ring_copy(0, steps, j_a).wait_recv()
            ring_copy(1, steps, j_b).wait_recv()

        near = jnp.where(at_last, steps, jnp.where(at_first, 0, s))
        prepare(xs_a, rs_a, wrap(me_z + zs - near, zs), piece(j_a))
        add(xs_b, rs_b)
        prepare(xs_b, rs_b, wrap(me_z + near, zs), piece(j_b))
        add(xs_a, rs_a)

    add(xs_b, rs_b)

    rows = TX * here
    swap = send(acc.at[pl.ds(rows, rows)], got, one_s.at[0], one_r.at[0], {"dom": twin})
    swap.start()
    swap.wait()
    logits = (acc[0:rows] + got[...]).reshape(TX, here, TY * columns)
    top = jnp.max(jnp.max(logits, axis=0), axis=1, keepdims=True)
    grown = jnp.sum(jnp.exp(logits - top[None]), axis=0)
    lane = lax.broadcasted_iota(jnp.int32, (here, TY * columns), 1)
    of_class = (lane // zs) % classes
    sums = [jnp.sum(jnp.where(of_class == k, grown, 0.0), axis=1, keepdims=True) for k in range(classes)]
    total = sums[0]
    for k in range(1, classes):
        total = total + sums[k]

    lane = lax.broadcasted_iota(jnp.int32, (here, 128), 1)
    fields = jnp.zeros((here, 128), F32)
    for n, v in enumerate((*sums, top, total, fixed, oid.astype(F32))):
        fields = jnp.where(lane == n, v, fields)
    fields = jnp.concatenate([fields, jnp.zeros((128 - here, 128), F32)], axis=0).T
    kinds = 2 * classes
    stat[...] = jnp.sum(pltpu.roll(fields[0:kinds], 0, 1, stride=here, stride_axis=0), axis=0, keepdims=True)

    def stat_copy(far, i):
        to = {"dom": wrap(me_d + i, doms), "cls": other} if far else {"dom": wrap(me_d + i, doms)}
        return send(stat, stat_in.at[me_c, me_d], mix_s.at[far, i], mix_r.at[far, i], to)

    @pl.loop(0, doms)
    def _(i):
        stat_copy(1, i).start()

        @pl.when(i > 0)
        def _():
            stat_copy(0, i).start()

    stat_in[me_c, me_d] = stat[...]

    @pl.loop(1, half)
    def _(i):
        row_copy(i).wait()

    @pl.loop(half, doms)
    def _(i):
        part_copy(i, 0).wait()
        part_copy(i, 1).wait()

    @pl.loop(0, doms)
    def _(i):
        stat_copy(1, i).wait()

        @pl.when(i > 0)
        def _():
            stat_copy(0, i).wait()

    packs = 128 // here
    of_sender = lax.broadcasted_iota(jnp.int32, (packs, 128), 1) // here == lax.broadcasted_iota(
        jnp.int32, (packs, 128), 0
    )

    def unpacked(c, names):
        tiles = [stat_in[c, n : n + packs].reshape(packs, 128) for n in range(0, doms, packs)]

        def field(f):
            turned = [pltpu.roll(v, (128 - f * here) % 128, 1) for v in tiles]
            turned = [pltpu.roll(v, 0, 1, stride=here, stride_axis=0) for v in turned]
            return jnp.concatenate(
                [jnp.sum(jnp.where(of_sender, v, 0.0), axis=0, keepdims=True) for v in turned], axis=1
            )

        return [field(f) for f in names]

    def norm(top_a, total_a, top_b, total_b):
        both = jnp.maximum(top_a, top_b)
        scale = jnp.exp(top_a - both)
        return scale, total_a * scale + total_b * jnp.exp(top_b - both)

    *mine, top_a, total_a, fixed_a, oid_a = unpacked(me_c, range(kinds))
    scale, total = norm(top_a, total_a, *unpacked(other, (classes, classes + 1)))
    mine = jnp.concatenate(mine, axis=0)
    weight = (fixed_a * (mine * scale / total)).astype(BF16).astype(F32)
    wide = 2 * classes
    of_entry = jnp.broadcast_to(oid_a.astype(jnp.int32), (wide, doms * here))
    none = jnp.zeros_like(weight)

    def grow(part):
        rows = jnp.concatenate([weight, none] if part == 0 else [none, weight], axis=0)
        mixing = jnp.concatenate([jnp.where(of_entry == o, rows, 0.0) for o in range(zs)], axis=0)
        return jnp.dot(
            mixing.astype(BF16), in_rows[part].reshape(doms * here, band), preferred_element_type=F32
        )

    volume = grow(0) + grow(1)
    for o in range(zs):
        slab[o] = volume[o * wide : (o + 1) * wide].astype(BF16)

    def z_copy(i):
        return send(slab.at[wrap(me_z + i, zs)], slab_in.at[i], z_s.at[i], z_r.at[i], {"orient": wrap(me_z + i, zs)})

    for i in sorted(range(1, zs), key=lambda i: -min(i, zs - i)):
        z_copy(i).start()

    slab_in[0] = slab[me_z]
    own, far = stat[...], stat_in[other, me_d]
    cut = lambda row, f: row[:, f * here : (f + 1) * here]
    scale, total = norm(cut(own, classes), cut(own, classes + 1), cut(far, classes), cut(far, classes + 1))
    for k in range(classes):
        prob_out[k : k + 1, :] = cut(own, k) * scale / total

    @pl.loop(1, half)
    def _(j):
        plane_copy(j).wait_send()

    @pl.loop(0, steps * half)
    def _(n):
        s = 1 + lax.div(n, half)
        j = n - half * (s - 1)

        @pl.when((s < steps) | (j < half // 2))
        def _():
            ring_copy(0, s, j).wait_send()

        @pl.when((s < steps) | (j >= half // 2))
        def _():
            ring_copy(1, s, j).wait_send()

    @pl.loop(1, zs)
    def _(i):
        z_copy(i).wait()

    out = slab_in[0].astype(F32)
    for i in range(1, zs):
        out = out + slab_in[i].astype(F32)
    vol_out[...] = out


def tables():
    kx = np.arange(IMG) - IMG // 2
    ky = np.arange(IMG // 2)
    turn_x = 2 * np.pi / IMG * ((np.arange(TX) - TX // 2)[:, None] * kx[None, :])
    turn_y = 2 * np.pi / IMG * (ky[:, None] * (np.arange(TY) - TY // 2)[None, :])
    return [
        np.stack([np.cos(t), np.sin(t)]).astype(np.float32) for t in (turn_x, turn_y.reshape(-1))
    ]


def solution(mesh):
    doms, zs = mesh.shape["dom"], mesh.shape["orient"]

    def local(references, images, orient_lists, shift_ids, fixed_weights):
        classes, here = references.shape[1], images.shape[1]
        columns = classes * references.shape[2]
        band = images.shape[2] // doms
        half = doms // 2
        vmem, hbm = pl.BlockSpec(memory_space=pltpu.VMEM), pl.BlockSpec(memory_space=pltpu.MemorySpace.HBM)
        dma = pltpu.SemaphoreType.DMA
        rows = TX * here
        prob, volume = pl.pallas_call(
            functools.partial(kernel, doms, zs),
            out_shape=(
                jax.ShapeDtypeStruct((classes, here), F32),
                jax.ShapeDtypeStruct((2 * classes, band), F32),
            ),
            in_specs=[hbm] * 7,
            out_specs=(vmem, vmem),
            scratch_shapes=[
                pltpu.VMEM((2, here, images.shape[2]), BF16),
                pltpu.VMEM((2, TX, IMG), F32),
                pltpu.SMEM((2, IMG // 2 * TY), F32),
                pltpu.VMEM((1, here), jnp.int32),
                pltpu.VMEM((1, here), jnp.int32),
                pltpu.VMEM((1, here), F32),
                pltpu.VMEM((zs, half, 2, columns, IMG), BF16),
                pltpu.VMEM((half, 2, here, band), BF16),
                pltpu.VMEM((doms, 2, here, band), BF16),
                pltpu.VMEM((2, doms, here, band), BF16),
                pltpu.VMEM((2 * rows, 2 * IMG), BF16),
                pltpu.VMEM((TY * columns, 2 * IMG), BF16),
                pltpu.VMEM((2 * rows, 2 * IMG), BF16),
                pltpu.VMEM((TY * columns, 2 * IMG), BF16),
                pltpu.VMEM((2 * rows, TY * columns), F32),
                pltpu.VMEM((rows, TY * columns), F32),
                pltpu.VMEM((1, 128), F32),
                pltpu.VMEM((2, doms, 1, 128), F32),
                pltpu.VMEM((zs, 2 * classes, band), BF16),
                pltpu.VMEM((zs, 2 * classes, band), BF16),
                dma((half,)), dma((half,)),
                dma((half,)), dma((half,)),
                dma((doms + half,)), dma((doms + half,)),
                dma((2, zs // 2, half)), dma((2, zs // 2, half)),
                dma((1,)), dma((1,)),
                dma((2, doms)), dma((2, doms)),
                dma((zs,)), dma((zs,)),
                dma((7,)),
            ],
            compiler_params=pltpu.CompilerParams(
                collective_id=0, has_side_effects=True, vmem_limit_bytes=48 << 20
            ),
            name="estep",
        )(
            *[
                pltpu.with_memory_space_constraint(v, pltpu.MemorySpace.HBM)
                for v in (
                    references.reshape(2, columns, references.shape[3]),
                    images,
                    *[jnp.asarray(t) for t in tables()],
                    orient_lists.reshape(1, here),
                    shift_ids.reshape(1, here),
                    fixed_weights.reshape(1, here),
                )
            ]
        )
        return prob.T, volume.reshape(2, classes, 1, band)

    in_specs = (
        P(None, "cls", None, ("dom", "orient")),
        P(None, ("dom", "orient"), None),
        P(("dom", "orient"), None),
        P(("dom", "orient"), None),
        P(("dom", "orient"), None),
    )
    out_specs = (P(("dom", "orient"), "cls"), P(None, "cls", "orient", "dom"))
    return jax.shard_map(local, mesh=mesh, in_specs=in_specs, out_specs=out_specs, check_vma=False)
```
